32 devices in a mesh: grp: 2 (over y), pts: 8 (over z, x), rcv: 2 (over core).
Axes of the slice: x: 2, y: 2, z: 4, core: 2. Of those that a mesh axis runs over, the one named last changes fastest.
Arguments:
- src_green: float32 [2, 128, 2048], P(None, 'grp', 'pts'), parts along dimension 1, may hold values from -0.125 to 0.125
- rcv_green: float32 [2, 2048, 2048], P(None, ('grp', 'rcv'), 'pts'), parts along dimension 1, may hold values from -6 to 6
- model: float32 [4096], P(('grp', 'pts')), parts along dimension 0, may hold values from -6 to 6
- observed: float32 [128, 2, 1024], P(('grp', 'pts'), None, 'rcv'), parts along dimension 0, may hold values from -30 to 30, as said below
Outputs:
- gradient: float32 [4096], P(('grp', 'pts')), parts along dimension 0
The draws below stay inside these ranges and needn't reach their ends.
There are 2 independent parts, one for each index of `grp`. The reference program is written for one: setup_inputs(seed, part) draws one part's arguments, and reference() takes and returns one part's arrays. A program takes and returns all parts, laid end to end along the dimension named above; each array names one. Nothing has to cross between parts.
Inputs may be any that keep to these rules, and one draw needn't show every extreme that they name: `observed`: complex data (real and imaginary parts) whose scale varies with the source.
All inputs are finite; a program needn't handle non-finite values.
Results may differ from the reference program's by a relative error of at most 0.000068.
Values sent between devices are 32-bit elements; how exact they have to be, the bound alone decides.
A program may use at most 64 MiB of HBM per device.

```python
import jax
import jax.numpy as jnp
from jax import lax

POINTS = 2048
RECEIVERS = 1024
SOURCES = 64


def draw_observed(key, part):
    key_base, key_jitter = jax.random.split(jax.random.fold_in(key, 7), 2)
    ramp = 3.0 ** (jnp.arange(SOURCES, dtype=jnp.float32) / SOURCES)
    ramp = ramp.reshape(SOURCES, 1, 1)
    jitter = jax.random.uniform(key_jitter, (SOURCES, 1, 1), jnp.float32, 0.7, 1.4)
    base = jnp.clip(jax.random.normal(key_base, (SOURCES, 2, RECEIVERS), jnp.float32), -6.0, 6.0) * 0.5
    return (base * ramp * jitter).astype(jnp.float32)


def shard_levels(own_key, shape, cuts, low, top_value):
    gain = 1.0
    for position, shards_of in cuts:
        draws = jax.random.uniform(jax.random.fold_in(jax.random.fold_in(own_key, 6), position), (shards_of,), jnp.float32, low / len(cuts), top_value / len(cuts))
        gain = gain * jnp.repeat(jnp.exp(draws), shape[position] // shards_of).reshape((-1,) + (1,) * (len(shape) - 1 - position))
    return gain


def scatter_about(rng, extent, width, most, pieces=(), kind=jnp.bfloat16):
    factor_of = shard_levels(rng, extent, pieces, -0.22, 0.18) if pieces else 1.0
    drawn = jax.random.normal(rng, extent, jnp.float32) * width * factor_of
    return jnp.minimum(jnp.maximum(drawn, -most), most).astype(kind)


def setup_inputs(seed: int = 0, part: int = 0) -> dict:
    key_of = jax.random.split(jax.random.key(seed), 5)
    part_splits = jax.random.split(jax.random.fold_in(key_of[4], part), 5)
    src_green = scatter_about(part_splits[0], (2, SOURCES, POINTS), POINTS ** -0.5, 0.125, ((2, 8),), jnp.float32)
    rcv_green = scatter_about(part_splits[1], (2, RECEIVERS, POINTS), 1.0, 6.0, ((1, 2), (2, 8)), jnp.float32)
    model = scatter_about(part_splits[2], (POINTS,), 1.0, 6.0, ((0, 8),), jnp.float32)
    observed = draw_observed(jax.random.fold_in(jax.random.fold_in(key_of[4], part), 71), part)
    return dict(src_green=src_green, rcv_green=rcv_green, model=model, observed=observed)


def modelled_data(scaled, rcv_green):
    highest = lax.Precision.HIGHEST
    real_part = jnp.dot(scaled[0], rcv_green[0].T, precision=highest, preferred_element_type=jnp.float32) - jnp.dot(scaled[1], rcv_green[1].T, precision=highest, preferred_element_type=jnp.float32)
    imag_part = jnp.dot(scaled[0], rcv_green[1].T, precision=highest, preferred_element_type=jnp.float32) + jnp.dot(scaled[1], rcv_green[0].T, precision=highest, preferred_element_type=jnp.float32)
    return jnp.stack([real_part, imag_part], axis=1)

def image_terms(weighted, rcv_green, src_rows):
    highest = lax.Precision.HIGHEST
    back_real = jnp.dot(weighted[:, 0, :], rcv_green[0], precision=highest, preferred_element_type=jnp.float32) + jnp.dot(weighted[:, 1, :], rcv_green[1], precision=highest, preferred_element_type=jnp.float32)
    back_imag = jnp.dot(weighted[:, 1, :], rcv_green[0], precision=highest, preferred_element_type=jnp.float32) - jnp.dot(weighted[:, 0, :], rcv_green[1], precision=highest, preferred_element_type=jnp.float32)
    return lax.optimization_barrier(jnp.sum(src_rows[0] * back_real + src_rows[1] * back_imag, axis=0))

def reference(src_green, rcv_green, model, observed):
    scaled = src_green * model[None, None, :]
    modelled = modelled_data(scaled, rcv_green)
    resid = modelled - observed
    energy = resid[:, 0, :] ** 2 + resid[:, 1, :] ** 2
    spread_sq = jnp.sum(energy) / (SOURCES * RECEIVERS) + 1e-06
    weighted = resid / (1.0 + energy / spread_sq)[:, None, :]
    gradient = image_terms(weighted, rcv_green, src_green)
    return gradient * jnp.sqrt(jnp.float32(POINTS) / (RECEIVERS * SOURCES))
```

```python
import functools
import math

import jax
import jax.numpy as jnp
from jax import lax
from jax.experimental import pallas as pl
from jax.experimental.pallas import tpu as pltpu
from jax.sharding import PartitionSpec as P

MESH = pl.DeviceIdType.MESH
UNROLL = 16
GROUP = 8


def split(a):
    high = a.astype(jnp.bfloat16)
    low = (a - high.astype(jnp.float32)).astype(jnp.bfloat16)
    return high, low


def product(a, b_high, b_low, b_axis):
    rows = a.shape[0]
    a_high, a_low = split(a)
    dims = (((1,), (b_axis,)), ((), ()))
    both = lax.dot_general(
        jnp.concatenate([a_high, a_low], axis=0), b_high, dims, preferred_element_type=jnp.float32
    )
    cross = lax.dot_general(a_high, b_low, dims, preferred_element_type=jnp.float32)
    return both[:rows] + (both[rows:] + cross)


def kernel(
    n, nr, scale,
    src_hbm, rcv_hbm, model_hbm, obs_hbm, out_ref,
    src, rcv, model, obs, b_high, b_low, part, rbuf, gath, own_energy, ebuf, img, img_in,
    load, rs, rr, gs, gr, es, er, ims, imr,
):
    p = lax.axis_index("pts")
    c = lax.axis_index("rcv")
    total = n * nr
    sources = src.shape[1]
    receivers = rcv.shape[1]
    chunks, _, _, block, width = part.shape
    halves = max(chunks // 2, 1)
    per_half = chunks // halves
    half = per_half * width
    paired = n <= UNROLL and n & (n - 1) == 0
    group = GROUP if n % GROUP == 0 else 1

    def peer(o):
        if not paired:
            return (p + o) % n
        q, bit = p, 1
        while bit < n:
            if o & bit:
                q = q + bit * (1 - 2 * ((p // bit) % 2))
            bit *= 2
        return q

    def origin(o):
        return peer(o) if paired else (p + n - o) % n

    def each(start, stop, body, far_first=True):
        if stop - start <= UNROLL:
            order = range(start, stop)
            for o in reversed(order) if far_first else order:
                body(o)
        else:

            @pl.loop(start, stop)
            def _(o):
                body(o)

    loads = [
        pltpu.make_async_copy(src_hbm, src, load.at[0]),
        pltpu.make_async_copy(model_hbm, model, load.at[1]),
    ]
    for h in range(halves):
        for i in range(2):
            loads.append(pltpu.make_async_copy(
                rcv_hbm.at[i, pl.ds(h * half, half)], rcv.at[i, pl.ds(h * half, half)], load.at[3 + 2 * h + i]
            ))
    obs_load = pltpu.make_async_copy(obs_hbm, obs, load.at[2])
    for copy in loads:
        copy.start()
    obs_load.start()

    barrier = pltpu.get_barrier_semaphore()
    q = p * nr + c

    def greet(o):
        to = (q + o) % total
        pl.semaphore_signal(
            barrier, inc=1, device_id={"pts": to // nr, "rcv": to % nr}, device_id_type=MESH
        )

    each(1, total, greet)

    loads[0].wait()
    loads[1].wait()

    def rows_from(part_of, first, device):
        return jnp.concatenate(
            [
                src[part_of, pl.ds(pl.multiple_of(device(first + i) * block, block), block)]
                for i in range(group)
            ],
            axis=0,
        )

    rows = group * block

    def send_sums(k):
        def send(o):
            pltpu.make_async_remote_copy(
                part.at[k, o], rbuf.at[k, o], rs.at[k], rr.at[k],
                device_id={"pts": peer(o)}, device_id_type=MESH,
            ).start()

        each(1, n, send)

    for h in range(halves):
        at = pl.ds(h * half, half)
        loads[2 + 2 * h].wait()
        b_high[0, at], b_low[0, at] = split(rcv[0, at])
        loads[3 + 2 * h].wait()
        b_high[1, at], b_low[1, at] = split(rcv[1, at])

        def forward(g):
            weight = model[...]
            scaled = jnp.concatenate(
                [rows_from(0, g * group, peer) * weight, rows_from(1, g * group, peer) * weight], axis=0
            )
            with_real = product(scaled, b_high[0, at], b_low[0, at], 1)
            with_imag = product(scaled, b_high[1, at], b_low[1, at], 1)
            real = (with_real[:rows] - with_imag[rows:]).reshape(group, block, half)
            imag = (with_imag[:rows] + with_real[rows:]).reshape(group, block, half)
            for j in range(per_half):
                k = h * per_half + j
                part[k, pl.ds(g * group, group), 0] = real[:, :, j * width:(j + 1) * width]
                part[k, pl.ds(g * group, group), 1] = imag[:, :, j * width:(j + 1) * width]

        each(0, n // group, forward)
        if h == 0:
            pl.semaphore_wait(barrier, total - 1)
        for j in range(per_half):
            send_sums(h * per_half + j)

    obs_load.wait()
    energy = jnp.zeros((block, width), jnp.float32)
    for k in range(chunks):
        arrived = rbuf.at[k, pl.ds(1, n - 1)]
        pltpu.make_async_copy(arrived, arrived, rr.at[k]).wait()
        at = pl.ds(k * width, width)
        resid = jnp.sum(rbuf[k, pl.ds(1, n - 1)], axis=0) + part[k, 0]
        real = resid[0] - obs[:, 0, at]
        imag = resid[1] - obs[:, 1, at]
        gath[k, 0, 0] = real
        gath[k, 0, 1] = imag
        energy = energy + (real * real + imag * imag)

        def spread(o):
            pltpu.make_async_remote_copy(
                gath.at[k, 0], gath.at[k, o], gs.at[k], gr.at[k],
                device_id={"pts": peer(o)}, device_id_type=MESH,
            ).start()

        each(1, n, spread)

    own_energy[0] = jnp.sum(energy, axis=0, keepdims=True)

    def tell(o):
        to = (q + o) % total
        pltpu.make_async_remote_copy(
            own_energy.at[0], ebuf.at[o - 1], es, er,
            device_id={"pts": to // nr, "rcv": to % nr}, device_id_type=MESH,
        ).start()

    each(1, total, tell)

    told = ebuf.at[pl.ds(0, total - 1)]
    pltpu.make_async_copy(told, told, er).wait()
    summed = jnp.sum(jnp.sum(ebuf[pl.ds(0, total - 1)], axis=0) + own_energy[0], axis=1, keepdims=True)
    spread_sq = summed / (sources * receivers * nr) + 1e-06
    inverse = 1.0 / spread_sq

    for k in range(chunks):
        arrived = gath.at[k, pl.ds(1, n - 1)]
        pltpu.make_async_copy(arrived, arrived, gr.at[k]).wait()

    def gathered(g, part_of):
        return jnp.concatenate(
            [gath[k, pl.ds(g * group, group), part_of].reshape(rows, width) for k in range(chunks)], axis=1
        )

    def image_of(g):
        real = gathered(g, 0)
        imag = gathered(g, 1)
        gain = 1.0 / (1.0 + (real * real + imag * imag) * inverse)
        weighted = jnp.concatenate([real * gain, imag * gain], axis=0)
        with_real = product(weighted, b_high[0], b_low[0], 0)
        with_imag = product(weighted, b_high[1], b_low[1], 0)
        back_real = with_real[:rows] + with_imag[rows:]
        back_imag = with_real[rows:] - with_imag[:rows]
        terms = rows_from(0, g * group, origin) * back_real + rows_from(1, g * group, origin) * back_imag
        return jnp.sum(terms, axis=0, keepdims=True)

    if n // group == 1:
        image = image_of(0)
    else:
        image = lax.fori_loop(
            0, n // group, lambda g, so_far: so_far + image_of(g), jnp.zeros((1, src.shape[2]), jnp.float32)
        )
    image = image * scale
    img[0] = image
    swaps = []
    for d in range(1, nr):
        copy = pltpu.make_async_remote_copy(
            img.at[0], img_in.at[d - 1], ims.at[d - 1], imr.at[d - 1],
            device_id={"rcv": (c + d) % nr}, device_id_type=MESH,
        )
        copy.start()
        swaps.append(copy)
    for k in range(chunks):
        sent = part.at[k, pl.ds(1, n - 1)]
        pltpu.make_async_copy(sent, sent, rs.at[k]).wait()
        spread_out = gath.at[k, pl.ds(1, n - 1)]
        pltpu.make_async_copy(spread_out, spread_out, gs.at[k]).wait()
    pltpu.make_async_copy(told, told, es).wait()
    for copy in swaps:
        copy.wait_recv()
    for d in range(1, nr):
        image = image + img_in[d - 1]
    out_ref[...] = image
    for copy in swaps:
        copy.wait_send()


def local(src_green, rcv_green, model, observed):
    n = lax.axis_size("pts")
    nr = lax.axis_size("rcv")
    sources, points = src_green.shape[1:]
    receivers = rcv_green.shape[1]
    block = observed.shape[0]
    scale = math.sqrt(points * n / (receivers * nr * sources))
    f32, bf16 = jnp.float32, jnp.bfloat16
    dma = pltpu.SemaphoreType.DMA
    width = 128 if receivers % 256 == 0 else receivers
    chunks = receivers // width
    blocks = (chunks, n, 2, block, width)
    image = pl.pallas_call(
        functools.partial(kernel, n, nr, scale),
        out_shape=jax.ShapeDtypeStruct((1, points), f32),
        in_specs=[pl.BlockSpec(memory_space=pl.ANY)] * 4,
        out_specs=pl.BlockSpec(memory_space=pltpu.VMEM),
        scratch_shapes=[
            pltpu.VMEM(src_green.shape, f32),
            pltpu.VMEM(rcv_green.shape, f32),
            pltpu.VMEM((1, points), f32),
            pltpu.VMEM(observed.shape, f32),
            pltpu.VMEM(rcv_green.shape, bf16),
            pltpu.VMEM(rcv_green.shape, bf16),
            pltpu.VMEM(blocks, f32),
            pltpu.VMEM(blocks, f32),
            pltpu.VMEM(blocks, f32),
            pltpu.VMEM((1, 1, width), f32),
            pltpu.VMEM((n * nr, 1, width), f32),
            pltpu.VMEM((1, 1, points), f32),
            pltpu.VMEM((max(nr - 1, 1), 1, points), f32),
            dma((3 + max(chunks, 2),)),
            dma((chunks,)),
            dma((chunks,)),
            dma((chunks,)),
            dma((chunks,)),
            dma(()),
            dma(()),
            dma((max(nr - 1, 1),)),
            dma((max(nr - 1, 1),)),
        ],
        compiler_params=pltpu.CompilerParams(collective_id=0, has_side_effects=True),
    )(src_green, rcv_green, model.reshape(1, points), observed)
    return image.reshape(points)


def solution(mesh):
    placed = (
        P(None, "grp", "pts"),
        P(None, ("grp", "rcv"), "pts"),
        P(("grp", "pts")),
        P(("grp", "pts"), None, "rcv"),
    )
    return jax.shard_map(
        local, mesh=mesh, in_specs=placed, out_specs=P(("grp", "pts")), check_vma=False
    )
```

```python
import functools
import math

import jax
import jax.numpy as jnp
from jax import lax
from jax.experimental import pallas as pl
from jax.experimental.pallas import tpu as pltpu
from jax.sharding import PartitionSpec as P

MESH = pl.DeviceIdType.MESH
UNROLL = 16
GROUP = 8


def split(a):
    high = a.astype(jnp.bfloat16)
    low = (a - high.astype(jnp.float32)).astype(jnp.bfloat16)
    return high, low


def product(a, b_high, b_low, b_axis):
    rows = a.shape[0]
    a_high, a_low = split(a)
    dims = (((1,), (b_axis,)), ((), ()))
    both = lax.dot_general(
        jnp.concatenate([a_high, a_low], axis=0), b_high, dims, preferred_element_type=jnp.float32
    )
    cross = lax.dot_general(a_high, b_low, dims, preferred_element_type=jnp.float32)
    return both[:rows] + (both[rows:] + cross)


def kernel(
    n, nr, scale,
    src_hbm, rcv_hbm, model_hbm, obs_hbm, out_ref,
    src, rcv, model, obs, b_high, b_low, part, rbuf, gath, zsend, zbuf, obst,
    own_energy, ebuf, img, img_in,
    load, rs, rr, gs, gr, zs, zr, es, er, ims, imr,
):
    p = lax.axis_index("pts")
    c = lax.axis_index("rcv")
    sources = src.shape[1]
    receivers = rcv.shape[1]
    chunks, m, sides, _, block, width = part.shape
    side, place = p // m, p % m
    total = m * nr
    halves = max(chunks // 2, 1)
    per_half = chunks // halves
    half = per_half * width
    paired = m <= UNROLL and m & (m - 1) == 0
    group = GROUP // sides if m % (GROUP // sides) == 0 else 1

    def peer(o):
        if not paired:
            return (place + o) % m
        q, bit = place, 1
        while bit < m:
            if o & bit:
                q = q + bit * (1 - 2 * ((place // bit) % 2))
            bit *= 2
        return q

    def origin(o):
        return peer(o) if paired else (place + m - o) % m

    def across(to):
        to = to % total
        return {"pts": side * m + to // nr, "rcv": to % nr}

    def each(start, stop, body, far_first=True):
        if stop - start <= UNROLL:
            order = range(start, stop)
            for o in reversed(order) if far_first else order:
                body(o)
        else:

            @pl.loop(start, stop)
            def _(o):
                body(o)

    loads = [
        pltpu.make_async_copy(src_hbm, src, load.at[0]),
        pltpu.make_async_copy(model_hbm, model, load.at[1]),
    ]
    for h in range(halves):
        for i in range(2):
            loads.append(pltpu.make_async_copy(
                rcv_hbm.at[i, pl.ds(h * half, half)], rcv.at[i, pl.ds(h * half, half)], load.at[3 + 2 * h + i]
            ))
    obs_load = pltpu.make_async_copy(obs_hbm, obs, load.at[2])
    for copy in loads:
        copy.start()
    obs_load.start()

    barrier = pltpu.get_barrier_semaphore()
    q = place * nr + c
    partners = [((side + t) % sides) * m + place for t in range(1, sides)]

    def greet(o):
        pl.semaphore_signal(barrier, inc=1, device_id=across(q + o), device_id_type=MESH)

    each(1, total, greet)
    for partner in partners:
        pl.semaphore_signal(barrier, inc=1, device_id={"pts": partner}, device_id_type=MESH)

    loads[0].wait()
    loads[1].wait()

    def rows_from(part_of, first, device):
        return jnp.concatenate(
            [
                src[part_of, pl.ds(pl.multiple_of((t * m + device(first + i)) * block, block), block)]
                for i in range(group)
                for t in range(sides)
            ],
            axis=0,
        )

    rows = group * sides * block

    def send_sums(k):
        def send(o):
            pltpu.make_async_remote_copy(
                part.at[k, o], rbuf.at[k, o], rs.at[k], rr.at[k],
                device_id={"pts": side * m + peer(o)}, device_id_type=MESH,
            ).start()

        each(1, m, send)

    for h in range(halves):
        at = pl.ds(h * half, half)
        loads[2 + 2 * h].wait()
        b_high[0, at], b_low[0, at] = split(rcv[0, at])
        loads[3 + 2 * h].wait()
        b_high[1, at], b_low[1, at] = split(rcv[1, at])

        def forward(g):
            weight = model[...]
            scaled = jnp.concatenate(
                [rows_from(0, g * group, peer) * weight, rows_from(1, g * group, peer) * weight], axis=0
            )
            with_real = product(scaled, b_high[0, at], b_low[0, at], 1)
            with_imag = product(scaled, b_high[1, at], b_low[1, at], 1)
            real = (with_real[:rows] - with_imag[rows:]).reshape(group, sides, block, half)
            imag = (with_imag[:rows] + with_real[rows:]).reshape(group, sides, block, half)
            for j in range(per_half):
                k = h * per_half + j
                part[k, pl.ds(g * group, group), :, 0] = real[..., j * width:(j + 1) * width]
                part[k, pl.ds(g * group, group), :, 1] = imag[..., j * width:(j + 1) * width]

        each(0, m // group, forward)
        if h == 0:
            pl.semaphore_wait(barrier, total - 1 + len(partners))
        for j in range(per_half):
            send_sums(h * per_half + j)

    obs_load.wait()
    for t in range(sides):
        for i in range(2):
            mine = jnp.where(side == t, obs[:, i, :], 0.0)
            for k in range(chunks):
                obst[k, t, i] = mine[:, k * width:(k + 1) * width]

    swaps = []
    for k in range(chunks):
        arrived = rbuf.at[k, pl.ds(1, m - 1)]
        pltpu.make_async_copy(arrived, arrived, rr.at[k]).wait()
        zsend[k] = jnp.sum(rbuf[k, pl.ds(1, m - 1)], axis=0) + (part[k, 0] - obst[k])
        for t, partner in enumerate(partners):
            copy = pltpu.make_async_remote_copy(
                zsend.at[k], zbuf.at[t, k], zs.at[t, k], zr.at[t, k],
                device_id={"pts": partner}, device_id_type=MESH,
            )
            copy.start()
            swaps.append(copy)

    energy = jnp.zeros((block, width), jnp.float32)
    for k in range(chunks):
        resid = zsend[k]
        for t in range(len(partners)):
            swaps[k * len(partners) + t].wait_recv()
            resid = resid + zbuf[t, k]
        gath[k, 0] = resid
        energy = energy + jnp.sum(jnp.sum(resid * resid, axis=0), axis=0)

        def spread(o):
            pltpu.make_async_remote_copy(
                gath.at[k, 0], gath.at[k, o], gs.at[k], gr.at[k],
                device_id={"pts": side * m + peer(o)}, device_id_type=MESH,
            ).start()

        each(1, m, spread)

    own_energy[0] = jnp.sum(energy, axis=0, keepdims=True)

    def tell(o):
        pltpu.make_async_remote_copy(
            own_energy.at[0], ebuf.at[o - 1], es, er, device_id=across(q + o), device_id_type=MESH
        ).start()

    each(1, total, tell)

    told = ebuf.at[pl.ds(0, total - 1)]
    pltpu.make_async_copy(told, told, er).wait()
    summed = jnp.sum(jnp.sum(ebuf[pl.ds(0, total - 1)], axis=0) + own_energy[0], axis=1, keepdims=True)
    spread_sq = summed / (sources * receivers * nr) + 1e-06
    inverse = 1.0 / spread_sq

    for k in range(chunks):
        arrived = gath.at[k, pl.ds(1, m - 1)]
        pltpu.make_async_copy(arrived, arrived, gr.at[k]).wait()

    def gathered(g, part_of):
        return jnp.concatenate(
            [gath[k, pl.ds(g * group, group), :, part_of].reshape(rows, width) for k in range(chunks)], axis=1
        )

    def image_of(g):
        real = gathered(g, 0)
        imag = gathered(g, 1)
        gain = 1.0 / (1.0 + (real * real + imag * imag) * inverse)
        weighted = jnp.concatenate([real * gain, imag * gain], axis=0)
        with_real = product(weighted, b_high[0], b_low[0], 0)
        with_imag = product(weighted, b_high[1], b_low[1], 0)
        back_real = with_real[:rows] + with_imag[rows:]
        back_imag = with_real[rows:] - with_imag[:rows]
        terms = rows_from(0, g * group, origin) * back_real + rows_from(1, g * group, origin) * back_imag
        return jnp.sum(terms, axis=0, keepdims=True)

    if m // group == 1:
        image = image_of(0)
    else:
        image = lax.fori_loop(
            0, m // group, lambda g, so_far: so_far + image_of(g), jnp.zeros((1, src.shape[2]), jnp.float32)
        )
    image = image * scale
    img[0] = image
    sums = []
    for d in range(1, nr):
        copy = pltpu.make_async_remote_copy(
            img.at[0], img_in.at[d - 1], ims.at[d - 1], imr.at[d - 1],
            device_id={"rcv": (c + d) % nr}, device_id_type=MESH,
        )
        copy.start()
        sums.append(copy)
    for k in range(chunks):
        sent = part.at[k, pl.ds(1, m - 1)]
        pltpu.make_async_copy(sent, sent, rs.at[k]).wait()
        spread_out = gath.at[k, pl.ds(1, m - 1)]
        pltpu.make_async_copy(spread_out, spread_out, gs.at[k]).wait()
    pltpu.make_async_copy(told, told, es).wait()
    for copy in swaps:
        copy.wait_send()
    for copy in sums:
        copy.wait_recv()
    for d in range(1, nr):
        image = image + img_in[d - 1]
    out_ref[...] = image
    for copy in sums:
        copy.wait_send()


def local(src_green, rcv_green, model, observed):
    n = lax.axis_size("pts")
    nr = lax.axis_size("rcv")
    sources, points = src_green.shape[1:]
    receivers = rcv_green.shape[1]
    block = observed.shape[0]
    scale = math.sqrt(points * n / (receivers * nr * sources))
    f32, bf16 = jnp.float32, jnp.bfloat16
    dma = pltpu.SemaphoreType.DMA
    width = 128 if receivers % 256 == 0 else receivers
    chunks = receivers // width
    sides = 2 if n % 2 == 0 and n > 2 else 1
    m = n // sides
    blocks = (chunks, m, sides, 2, block, width)
    swapped = (max(sides - 1, 1), chunks, sides, 2, block, width)
    image = pl.pallas_call(
        functools.partial(kernel, n, nr, scale),
        out_shape=jax.ShapeDtypeStruct((1, points), f32),
        in_specs=[pl.BlockSpec(memory_space=pl.ANY)] * 4,
        out_specs=pl.BlockSpec(memory_space=pltpu.VMEM),
        scratch_shapes=[
            pltpu.VMEM(src_green.shape, f32),
            pltpu.VMEM(rcv_green.shape, f32),
            pltpu.VMEM((1, points), f32),
            pltpu.VMEM(observed.shape, f32),
            pltpu.VMEM(rcv_green.shape, bf16),
            pltpu.VMEM(rcv_green.shape, bf16),
            pltpu.VMEM(blocks, f32),
            pltpu.VMEM(blocks, f32),
            pltpu.VMEM(blocks, f32),
            pltpu.VMEM(swapped[1:], f32),
            pltpu.VMEM(swapped, f32),
            pltpu.VMEM(swapped[1:], f32),
            pltpu.VMEM((1, 1, width), f32),
            pltpu.VMEM((m * nr, 1, width), f32),
            pltpu.VMEM((1, 1, points), f32),
            pltpu.VMEM((max(nr - 1, 1), 1, points), f32),
            dma((3 + max(chunks, 2),)),
            dma((chunks,)),
            dma((chunks,)),
            dma((chunks,)),
            dma((chunks,)),
            dma(swapped[:2]),
            dma(swapped[:2]),
            dma(()),
            dma(()),
            dma((max(nr - 1, 1),)),
            dma((max(nr - 1, 1),)),
        ],
        compiler_params=pltpu.CompilerParams(collective_id=0, has_side_effects=True),
    )(src_green, rcv_green, model.reshape(1, points), observed)
    return image.reshape(points)


def solution(mesh):
    placed = (
        P(None, "grp", "pts"),
        P(None, ("grp", "rcv"), "pts"),
        P(("grp", "pts")),
        P(("grp", "pts"), None, "rcv"),
    )
    return jax.shard_map(
        local, mesh=mesh, in_specs=placed, out_specs=P(("grp", "pts")), check_vma=False
    )
```

```python
import functools
import math

import jax
import jax.numpy as jnp
from jax import lax
from jax.experimental import pallas as pl
from jax.experimental.pallas import tpu as pltpu
from jax.sharding import PartitionSpec as P

MESH = pl.DeviceIdType.MESH
UNROLL = 16
GROUP = 8
VMEM = 56550500


def split(a):
    high = a.astype(jnp.bfloat16)
    low = (a - high.astype(jnp.float32)).astype(jnp.bfloat16)
    return high, low


def product(a, b_high, b_low, b_axis):
    rows = a.shape[0]
    a_high, a_low = split(a)
    dims = (((1,), (b_axis,)), ((), ()))
    both = lax.dot_general(
        jnp.concatenate([a_high, a_low], axis=0), b_high, dims, preferred_element_type=jnp.float32
    )
    cross = lax.dot_general(a_high, b_low, dims, preferred_element_type=jnp.float32)
    return both[:rows] + (both[rows:] + cross)


def kernel(
    n, nr, scale,
    src_hbm, rcv_hbm, model_hbm, obs_hbm, out_ref,
    src, rcv, model, obs, b_high, b_low, part, rbuf, zsend, zbuf, resid, gath, obst, img, img_in,
    load, rs, rr, gs, gr, zs, zr, ims, imr,
):
    p = lax.axis_index("pts")
    c = lax.axis_index("rcv")
    sources = src.shape[1]
    receivers = rcv.shape[1]
    chunks, m, sides, _, block, width = part.shape
    side, place = p // m, p % m
    owner = nr - 1
    owns = c == owner
    behind = owner - c
    halves = max(chunks // 2, 1)
    per_half = chunks // halves
    half = per_half * width
    paired = m <= UNROLL and m & (m - 1) == 0
    group = GROUP // sides if m % (GROUP // sides) == 0 else 1
    rows = group * sides * block
    tiles = 2 * sides

    def peer(o):
        if not paired:
            return (place + o) % m
        q, bit = place, 1
        while bit < m:
            if o & bit:
                q = q + bit * (1 - 2 * ((place // bit) % 2))
            bit *= 2
        return q

    def origin(o):
        return peer(o) if paired else (place + m - o) % m

    def at_core(o, core):
        return {"pts": side * m + peer(o), "rcv": core}

    def each(start, stop, body):
        if stop - start <= UNROLL:
            for o in reversed(range(start, stop)):
                body(o)
        else:

            @pl.loop(start, stop)
            def _(o):
                body(o)

    loads = [
        pltpu.make_async_copy(src_hbm, src, load.at[0]),
        pltpu.make_async_copy(model_hbm, model, load.at[1]),
    ]
    for h in range(halves):
        for i in range(2):
            loads.append(pltpu.make_async_copy(
                rcv_hbm.at[i, pl.ds(h * half, half)], rcv.at[i, pl.ds(h * half, half)], load.at[3 + 2 * h + i]
            ))
    obs_load = pltpu.make_async_copy(obs_hbm, obs, load.at[2])
    for copy in loads:
        copy.start()
    obs_load.start()

    barrier = pltpu.get_barrier_semaphore()
    partners = [((side + t) % sides) * m + place for t in range(1, sides)]

    def greet(device):
        pl.semaphore_signal(barrier, inc=1, device_id=device, device_id_type=MESH)

    def to_owner(o):
        greet(at_core(o, owner))

    each(1, m, to_owner)
    for d in range(1, nr):
        greet({"rcv": (c + d) % nr})

    @pl.when(owns)
    def _():
        for partner in partners:
            greet({"pts": partner})

        def to_others(o):
            for core in range(owner):
                greet(at_core(o, core))

        each(1, m, to_others)

    loads[0].wait()
    loads[1].wait()

    def rows_from(part_of, first, device):
        return jnp.concatenate(
            [
                src[part_of, pl.ds(pl.multiple_of((t * m + device(first + i)) * block, block), block)]
                for i in range(group)
                for t in range(sides)
            ],
            axis=0,
        )

    def sum_copy(k, o):
        return pltpu.make_async_remote_copy(
            part.at[k, o], rbuf.at[k, o * nr + behind], rs.at[k], rr.at[k],
            device_id=at_core(o, owner), device_id_type=MESH,
        )

    for h in range(halves):
        at = pl.ds(h * half, half)
        loads[2 + 2 * h].wait()
        b_high[0, at], b_low[0, at] = split(rcv[0, at])
        loads[3 + 2 * h].wait()
        b_high[1, at], b_low[1, at] = split(rcv[1, at])

        def forward(g):
            weight = model[...]
            scaled = jnp.concatenate(
                [rows_from(0, g * group, peer) * weight, rows_from(1, g * group, peer) * weight], axis=0
            )
            with_real = product(scaled, b_high[0, at], b_low[0, at], 1)
            with_imag = product(scaled, b_high[1, at], b_low[1, at], 1)
            real = (with_real[:rows] - with_imag[rows:]).reshape(group, sides, block, half)
            imag = (with_imag[:rows] + with_real[rows:]).reshape(group, sides, block, half)
            for j in range(per_half):
                k = h * per_half + j
                part[k, pl.ds(g * group, group), :, 0] = real[..., j * width:(j + 1) * width]
                part[k, pl.ds(g * group, group), :, 1] = imag[..., j * width:(j + 1) * width]

        each(0, m // group, forward)
        if h == 0:

            @pl.when(owns)
            def _():
                pl.semaphore_wait(barrier, m * nr - 1 + len(partners))

            @pl.when(jnp.logical_not(owns))
            def _():
                pl.semaphore_wait(barrier, m - 1 + nr - 1)

            obs_load.wait()
            for t in range(sides):
                for i in range(2):
                    mine = jnp.where(side == t, obs[:, i, :], 0.0)
                    for k in range(chunks):
                        obst[k, t, i] = mine[:, k * width:(k + 1) * width]
        for j in range(per_half):
            k = h * per_half + j
            each(1, m, lambda o: sum_copy(k, o).start())
            part[k, 0] = part[k, 0] - obst[k]
            pl.when(jnp.logical_not(owns))(sum_copy(k, 0).start)

    def swap(k, t):
        return pltpu.make_async_remote_copy(
            zsend.at[k], zbuf.at[t, k], zs.at[t, k], zr.at[t, k],
            device_id={"pts": partners[t]}, device_id_type=MESH,
        )

    def sent_tiles(k):
        return pl.ds(0, tiles + 1 if k == chunks - 1 else tiles)

    def residual_copy(k, o, core):
        return pltpu.make_async_remote_copy(
            resid.at[k, core, sent_tiles(k)], gath.at[k, o, sent_tiles(k)], gs.at[k], gr.at[k],
            device_id=at_core(o, core), device_id_type=MESH,
        )

    @pl.when(owns)
    def _():
        for k in range(chunks):
            arrived = rbuf.at[k, pl.ds(1, m * nr - 1)]
            pltpu.make_async_copy(arrived, arrived, rr.at[k]).wait()
            for core in range(nr):
                first = owner - core
                acc = part[k, 0] if core == owner else rbuf[k, first]
                if m <= UNROLL:
                    for o in range(1, m):
                        acc = acc + rbuf[k, o * nr + first]
                else:
                    acc = lax.fori_loop(1, m, lambda o, so_far: so_far + rbuf[k, o * nr + first], acc)
                zsend[k, core] = acc
            for t in range(len(partners)):
                swap(k, t).start()

        energy = jnp.zeros((block, width), jnp.float32)
        for k in range(chunks):
            for t in range(len(partners)):
                swap(k, t).wait_recv()
            for core in range(nr):
                whole = zsend[k, core]
                for t in range(len(partners)):
                    whole = whole + zbuf[t, k, core]
                whole = whole.reshape(tiles, block, width)
                resid[k, core, pl.ds(0, tiles)] = whole
                energy = energy + jnp.sum(whole * whole, axis=0)
            if k == chunks - 1:
                for core in range(nr):
                    resid[k, core, tiles] = energy

            def spread(o):
                for core in range(nr):
                    residual_copy(k, o, core).start()

            each(1, m, spread)
            for core in range(owner):
                residual_copy(k, 0, core).start()
            gath[k, 0, sent_tiles(k)] = resid[k, owner, sent_tiles(k)]

    def arrival(k, first):
        arrived = gath.at[k, pl.ds(first, m - first), sent_tiles(k)]
        return pltpu.make_async_copy(arrived, arrived, gr.at[k])

    for k in range(chunks):
        pl.when(owns)(arrival(k, 1).wait)
        pl.when(jnp.logical_not(owns))(arrival(k, 0).wait)
    summed = jnp.sum(jnp.sum(gath[chunks - 1, :, tiles], axis=0), axis=(0, 1), keepdims=True)
    spread_sq = summed / (sources * receivers * nr) + 1e-06
    inverse = 1.0 / spread_sq

    def gathered(g, part_of):
        return jnp.concatenate(
            [
                jnp.concatenate(
                    [
                        gath[k, g * group + i, 2 * t + part_of]
                        for i in range(group)
                        for t in range(sides)
                    ],
                    axis=0,
                )
                for k in range(chunks)
            ],
            axis=1,
        )

    def image_of(g):
        real = gathered(g, 0)
        imag = gathered(g, 1)
        gain = 1.0 / (1.0 + (real * real + imag * imag) * inverse)
        weighted = jnp.concatenate([real * gain, imag * gain], axis=0)
        with_real = product(weighted, b_high[0], b_low[0], 0)
        with_imag = product(weighted, b_high[1], b_low[1], 0)
        back_real = with_real[:rows] + with_imag[rows:]
        back_imag = with_real[rows:] - with_imag[:rows]
        terms = rows_from(0, g * group, origin) * back_real + rows_from(1, g * group, origin) * back_imag
        return jnp.sum(terms, axis=0, keepdims=True)

    if m // group == 1:
        image = image_of(0)
    else:
        image = lax.fori_loop(
            0, m // group, lambda g, so_far: so_far + image_of(g), jnp.zeros((1, src.shape[2]), jnp.float32)
        )
    image = image * scale
    img[0] = image
    sums = []
    for d in range(1, nr):
        copy = pltpu.make_async_remote_copy(
            img.at[0], img_in.at[d - 1], ims.at[d - 1], imr.at[d - 1],
            device_id={"rcv": (c + d) % nr}, device_id_type=MESH,
        )
        copy.start()
        sums.append(copy)

    def sums_left(k, first):
        sent = part.at[k, pl.ds(first, m - first)]
        return pltpu.make_async_copy(sent, sent, rs.at[k])

    def residuals_left(k):
        sent = gath.at[k, pl.ds(0, m * nr - 1), sent_tiles(k)]
        return pltpu.make_async_copy(sent, sent, gs.at[k])

    for k in range(chunks):
        pl.when(jnp.logical_not(owns))(sums_left(k, 0).wait)

    @pl.when(owns)
    def _():
        for k in range(chunks):
            sums_left(k, 1).wait()
            for t in range(len(partners)):
                swap(k, t).wait_send()
            residuals_left(k).wait()

    for copy in sums:
        copy.wait_recv()
    for d in range(1, nr):
        image = image + img_in[d - 1]
    out_ref[...] = image
    for copy in sums:
        copy.wait_send()


def local(src_green, rcv_green, model, observed):
    n = lax.axis_size("pts")
    nr = lax.axis_size("rcv")
    sources, points = src_green.shape[1:]
    receivers = rcv_green.shape[1]
    block = observed.shape[0]
    scale = math.sqrt(points * n / (receivers * nr * sources))
    f32, bf16 = jnp.float32, jnp.bfloat16
    dma = pltpu.SemaphoreType.DMA
    width = 128 if receivers % 256 == 0 else receivers
    chunks = receivers // width
    sides = 2 if n % 2 == 0 and n > 2 else 1
    m = n // sides
    blocks = (sides, 2, block, width)
    tiles = (2 * sides + 1, block, width)
    image = pl.pallas_call(
        functools.partial(kernel, n, nr, scale),
        out_shape=jax.ShapeDtypeStruct((1, points), f32),
        in_specs=[pl.BlockSpec(memory_space=pl.ANY)] * 4,
        out_specs=pl.BlockSpec(memory_space=pltpu.VMEM),
        scratch_shapes=[
            pltpu.VMEM(src_green.shape, f32),
            pltpu.VMEM(rcv_green.shape, f32),
            pltpu.VMEM((1, points), f32),
            pltpu.VMEM(observed.shape, f32),
            pltpu.VMEM(rcv_green.shape, bf16),
            pltpu.VMEM(rcv_green.shape, bf16),
            pltpu.VMEM((chunks, m) + blocks, f32),
            pltpu.VMEM((chunks, m * nr) + blocks, f32),
            pltpu.VMEM((chunks, nr) + blocks, f32),
            pltpu.VMEM((max(sides - 1, 1), chunks, nr) + blocks, f32),
            pltpu.VMEM((chunks, nr) + tiles, f32),
            pltpu.VMEM((chunks, m * nr) + tiles, f32),
            pltpu.VMEM((chunks,) + blocks, f32),
            pltpu.VMEM((1, 1, points), f32),
            pltpu.VMEM((max(nr - 1, 1), 1, points), f32),
            dma((3 + max(chunks, 2),)),
            dma((chunks,)),
            dma((chunks,)),
            dma((chunks,)),
            dma((chunks,)),
            dma((max(sides - 1, 1), chunks)),
            dma((max(sides - 1, 1), chunks)),
            dma((max(nr - 1, 1),)),
            dma((max(nr - 1, 1),)),
        ],
        compiler_params=pltpu.CompilerParams(collective_id=0, has_side_effects=True, vmem_limit_bytes=VMEM),
    )(src_green, rcv_green, model.reshape(1, points), observed)
    return image.reshape(points)


def solution(mesh):
    placed = (
        P(None, "grp", "pts"),
        P(None, ("grp", "rcv"), "pts"),
        P(("grp", "pts")),
        P(("grp", "pts"), None, "rcv"),
    )
    return jax.shard_map(
        local, mesh=mesh, in_specs=placed, out_specs=P(("grp", "pts")), check_vma=False
    )
```

```python
import functools
import math

import jax
import jax.numpy as jnp
from jax import lax
from jax.experimental import pallas as pl
from jax.experimental.pallas import tpu as pltpu
from jax.sharding import PartitionSpec as P

MESH = pl.DeviceIdType.MESH
UNROLL = 16
GROUP = 8
VMEM = 56550500


def split(a):
    high = a.astype(jnp.bfloat16)
    low = (a - high.astype(jnp.float32)).astype(jnp.bfloat16)
    return high, low


def product(a, b_high, b_low, b_axis):
    rows = a.shape[0]
    a_high, a_low = split(a)
    dims = (((1,), (b_axis,)), ((), ()))
    both = lax.dot_general(
        jnp.concatenate([a_high, a_low], axis=0), b_high, dims, preferred_element_type=jnp.float32
    )
    cross = lax.dot_general(a_high, b_low, dims, preferred_element_type=jnp.float32)
    return both[:rows] + (both[rows:] + cross)


def kernel(
    n, nr, scale,
    src_hbm, rcv_hbm, model_hbm, obs_hbm, out_ref,
    src, rcv, model, obs, b_high, b_low, part, rbuf, zsend, zbuf, resid, gath, obst, told, ebuf, img, img_in,
    load, rs, rr, gs, gr, zs, zr, es, er, ims, imr,
):
    p = lax.axis_index("pts")
    c = lax.axis_index("rcv")
    sources = src.shape[1]
    receivers = rcv.shape[1]
    chunks, m, sides, _, block, width = part.shape
    side, place = p // m, p % m
    owner = nr - 1
    owns = c == owner
    behind = owner - c
    last = sides - 1
    tells = jnp.logical_and(owns, side == last)
    halves = max(chunks // 2, 1)
    per_half = chunks // halves
    half = per_half * width
    paired = m <= UNROLL and m & (m - 1) == 0
    group = GROUP // sides if m % (GROUP // sides) == 0 else 1
    rows = group * sides * block
    tiles = 2 * sides

    def peer(o):
        if not paired:
            return (place + o) % m
        q, bit = place, 1
        while bit < m:
            if o & bit:
                q = q + bit * (1 - 2 * ((place // bit) % 2))
            bit *= 2
        return q

    def origin(o):
        return peer(o) if paired else (place + m - o) % m

    def at_core(o, core):
        return {"pts": side * m + peer(o), "rcv": core}

    def each(start, stop, body):
        if stop - start <= UNROLL:
            for o in reversed(range(start, stop)):
                body(o)
        else:

            @pl.loop(start, stop)
            def _(o):
                body(o)

    loads = [
        pltpu.make_async_copy(src_hbm, src, load.at[0]),
        pltpu.make_async_copy(model_hbm, model, load.at[1]),
    ]
    for h in range(halves):
        for i in range(2):
            loads.append(pltpu.make_async_copy(
                rcv_hbm.at[i, pl.ds(h * half, half)], rcv.at[i, pl.ds(h * half, half)], load.at[3 + 2 * h + i]
            ))
    obs_load = pltpu.make_async_copy(obs_hbm, obs, load.at[2])
    for copy in loads[2:4] + loads[:2] + loads[4:]:
        copy.start()
    obs_load.start()

    barrier = pltpu.get_barrier_semaphore()
    partners = [((side + t) % sides) * m + place for t in range(1, sides)]

    def greet(device):
        pl.semaphore_signal(barrier, inc=1, device_id=device, device_id_type=MESH)

    def to_owner(o):
        greet(at_core(o, owner))

    each(1, m, to_owner)
    for d in range(1, nr):
        greet({"rcv": (c + d) % nr})

    @pl.when(owns)
    def _():
        for partner in partners:
            greet({"pts": partner})

        def to_others(o):
            for core in range(owner):
                greet(at_core(o, core))

        each(1, m, to_others)

    @pl.when(side != last)
    def _():
        def to_teller(o):
            greet({"pts": last * m + peer(o), "rcv": owner})

        each(1, m, to_teller)
        pl.when(jnp.logical_not(owns))(functools.partial(to_teller, 0))

    loads[0].wait()
    loads[1].wait()

    def rows_from(part_of, first, device):
        return jnp.concatenate(
            [
                src[part_of, pl.ds(pl.multiple_of((t * m + device(first + i)) * block, block), block)]
                for i in range(group)
                for t in range(sides)
            ],
            axis=0,
        )

    def sum_copy(k, o):
        return pltpu.make_async_remote_copy(
            part.at[k, o], rbuf.at[k, o * nr + behind], rs.at[k], rr.at[k],
            device_id=at_core(o, owner), device_id_type=MESH,
        )

    for h in range(halves):
        at = pl.ds(h * half, half)
        loads[2 + 2 * h].wait()
        b_high[0, at], b_low[0, at] = split(rcv[0, at])
        loads[3 + 2 * h].wait()
        b_high[1, at], b_low[1, at] = split(rcv[1, at])

        def forward(g):
            weight = model[...]
            scaled = jnp.concatenate(
                [rows_from(0, g * group, peer) * weight, rows_from(1, g * group, peer) * weight], axis=0
            )
            with_real = product(scaled, b_high[0, at], b_low[0, at], 1)
            with_imag = product(scaled, b_high[1, at], b_low[1, at], 1)
            real = (with_real[:rows] - with_imag[rows:]).reshape(group, sides, block, half)
            imag = (with_imag[:rows] + with_real[rows:]).reshape(group, sides, block, half)
            for j in range(per_half):
                k = h * per_half + j
                part[k, pl.ds(g * group, group), :, 0] = real[..., j * width:(j + 1) * width]
                part[k, pl.ds(g * group, group), :, 1] = imag[..., j * width:(j + 1) * width]

        each(0, m // group, forward)
        if h == 0:

            @pl.when(jnp.logical_and(owns, side != last))
            def _():
                pl.semaphore_wait(barrier, m * nr - 1 + len(partners))

            @pl.when(tells)
            def _():
                pl.semaphore_wait(barrier, sides * m * nr - 1)

            @pl.when(jnp.logical_not(owns))
            def _():
                pl.semaphore_wait(barrier, m - 1 + nr - 1)

            obs_load.wait()
            for t in range(sides):
                for i in range(2):
                    mine = jnp.where(side == t, obs[:, i, :], 0.0)
                    for k in range(chunks):
                        obst[k, t, i] = mine[:, k * width:(k + 1) * width]
        for j in range(per_half):
            k = h * per_half + j
            each(1, m, lambda o: sum_copy(k, o).start())
            part[k, 0] = part[k, 0] - obst[k]
            pl.when(jnp.logical_not(owns))(sum_copy(k, 0).start)

    def swap(k, t):
        return pltpu.make_async_remote_copy(
            zsend.at[k], zbuf.at[t, k], zs.at[t, k], zr.at[t, k],
            device_id={"pts": partners[t]}, device_id_type=MESH,
        )

    def residual_copy(k, o, core):
        return pltpu.make_async_remote_copy(
            resid.at[k, core], gath.at[k, o], gs.at[k], gr.at[k],
            device_id=at_core(o, core), device_id_type=MESH,
        )

    def spread(k):
        def to_peer(o):
            for core in range(nr):
                residual_copy(k, o, core).start()

        each(1, m, to_peer)
        for core in range(owner):
            residual_copy(k, 0, core).start()

    @pl.when(owns)
    def _():
        for k in range(chunks):
            arrived = rbuf.at[k, pl.ds(1, m * nr - 1)]
            pltpu.make_async_copy(arrived, arrived, rr.at[k]).wait()
            for core in range(nr):
                first = owner - core
                acc = part[k, 0] if core == owner else rbuf[k, first]
                if m <= UNROLL:
                    for o in range(1, m):
                        acc = acc + rbuf[k, o * nr + first]
                else:
                    acc = lax.fori_loop(1, m, lambda o, so_far: so_far + rbuf[k, o * nr + first], acc)
                zsend[k, core] = acc
            for t in range(len(partners)):
                swap(k, t).start()

        energy = jnp.zeros((block, width), jnp.float32)
        for k in range(chunks):
            for t in range(len(partners)):
                swap(k, t).wait_recv()
            for core in range(nr):
                whole = zsend[k, core]
                for t in range(len(partners)):
                    whole = whole + zbuf[t, k, core]
                whole = whole.reshape(tiles, block, width)
                resid[k, core] = whole
                energy = energy + jnp.sum(whole * whole, axis=0)
            gath[k, 0] = resid[k, owner]
            pl.when(side != last)(functools.partial(spread, k))
        energy = jnp.sum(energy, axis=0, keepdims=True)

        @pl.when(side == last)
        def _():
            told[0] = energy
            ebuf[0] = energy

            def tell(o, own=False):
                for t in range(sides):
                    for core in range(nr):
                        if not (own and t == last and core == owner):
                            pltpu.make_async_remote_copy(
                                told.at[0], ebuf.at[o], es, er,
                                device_id={"pts": t * m + peer(o), "rcv": core}, device_id_type=MESH,
                            ).start()

            each(1, m, tell)
            tell(0, own=True)
            for k in range(chunks):
                spread(k)

    def arrival(k, first):
        arrived = gath.at[k, pl.ds(first, m - first)]
        return pltpu.make_async_copy(arrived, arrived, gr.at[k])

    def energies(first):
        heard = ebuf.at[pl.ds(first, m - first)]
        return pltpu.make_async_copy(heard, heard, er)

    pl.when(tells)(energies(1).wait)
    pl.when(jnp.logical_not(tells))(energies(0).wait)
    summed = jnp.sum(jnp.sum(ebuf[pl.ds(0, m)], axis=0), axis=(0, 1), keepdims=True)
    spread_sq = summed / (sources * receivers * nr) + 1e-06
    inverse = 1.0 / spread_sq

    def gathered(g, h, part_of):
        return jnp.concatenate(
            [
                jnp.concatenate(
                    [
                        gath[k, g * group + i, 2 * t + part_of]
                        for i in range(group)
                        for t in range(sides)
                    ],
                    axis=0,
                )
                for k in range(h * per_half, (h + 1) * per_half)
            ],
            axis=1,
        )

    def image_of(g, h):
        at = pl.ds(h * half, half)
        real = gathered(g, h, 0)
        imag = gathered(g, h, 1)
        gain = 1.0 / (1.0 + (real * real + imag * imag) * inverse)
        weighted = jnp.concatenate([real * gain, imag * gain], axis=0)
        with_real = product(weighted, b_high[0, at], b_low[0, at], 0)
        with_imag = product(weighted, b_high[1, at], b_low[1, at], 0)
        back_real = with_real[:rows] + with_imag[rows:]
        back_imag = with_real[rows:] - with_imag[:rows]
        terms = rows_from(0, g * group, origin) * back_real + rows_from(1, g * group, origin) * back_imag
        return jnp.sum(terms, axis=0, keepdims=True)

    image = jnp.zeros((1, src.shape[2]), jnp.float32)
    for h in range(halves):
        for k in range(h * per_half, (h + 1) * per_half):
            pl.when(owns)(arrival(k, 1).wait)
            pl.when(jnp.logical_not(owns))(arrival(k, 0).wait)
        if m // group == 1:
            image = image + image_of(0, h)
        else:
            image = lax.fori_loop(0, m // group, lambda g, so_far: so_far + image_of(g, h), image)
    image = image * scale
    img[0] = image
    sums = []
    for d in range(1, nr):
        copy = pltpu.make_async_remote_copy(
            img.at[0], img_in.at[d - 1], ims.at[d - 1], imr.at[d - 1],
            device_id={"rcv": (c + d) % nr}, device_id_type=MESH,
        )
        copy.start()
        sums.append(copy)

    def sums_left(k, first):
        sent = part.at[k, pl.ds(first, m - first)]
        return pltpu.make_async_copy(sent, sent, rs.at[k])

    def residuals_left(k):
        sent = gath.at[k, pl.ds(0, m * nr - 1)]
        return pltpu.make_async_copy(sent, sent, gs.at[k])

    for k in range(chunks):
        pl.when(jnp.logical_not(owns))(sums_left(k, 0).wait)

    @pl.when(owns)
    def _():
        for k in range(chunks):
            sums_left(k, 1).wait()
            for t in range(len(partners)):
                swap(k, t).wait_send()
            residuals_left(k).wait()

    @pl.when(tells)
    def _():
        every = ebuf.at[pl.ds(0, n * nr - 1)]
        pltpu.make_async_copy(every, every, es).wait()

    for copy in sums:
        copy.wait_recv()
    for d in range(1, nr):
        image = image + img_in[d - 1]
    out_ref[...] = image
    for copy in sums:
        copy.wait_send()


def local(src_green, rcv_green, model, observed):
    n = lax.axis_size("pts")
    nr = lax.axis_size("rcv")
    sources, points = src_green.shape[1:]
    receivers = rcv_green.shape[1]
    block = observed.shape[0]
    scale = math.sqrt(points * n / (receivers * nr * sources))
    f32, bf16 = jnp.float32, jnp.bfloat16
    dma = pltpu.SemaphoreType.DMA
    width = 128 if receivers % 256 == 0 else receivers
    chunks = receivers // width
    sides = 2 if n % 2 == 0 and n > 2 else 1
    m = n // sides
    blocks = (sides, 2, block, width)
    tiles = (2 * sides, block, width)
    image = pl.pallas_call(
        functools.partial(kernel, n, nr, scale),
        out_shape=jax.ShapeDtypeStruct((1, points), f32),
        in_specs=[pl.BlockSpec(memory_space=pl.ANY)] * 4,
        out_specs=pl.BlockSpec(memory_space=pltpu.VMEM),
        scratch_shapes=[
            pltpu.VMEM(src_green.shape, f32),
            pltpu.VMEM(rcv_green.shape, f32),
            pltpu.VMEM((1, points), f32),
            pltpu.VMEM(observed.shape, f32),
            pltpu.VMEM(rcv_green.shape, bf16),
            pltpu.VMEM(rcv_green.shape, bf16),
            pltpu.VMEM((chunks, m) + blocks, f32),
            pltpu.VMEM((chunks, m * nr) + blocks, f32),
            pltpu.VMEM((chunks, nr) + blocks, f32),
            pltpu.VMEM((max(sides - 1, 1), chunks, nr) + blocks, f32),
            pltpu.VMEM((chunks, nr) + tiles, f32),
            pltpu.VMEM((chunks, m * nr) + tiles, f32),
            pltpu.VMEM((chunks,) + blocks, f32),
            pltpu.VMEM((1, 1, width), f32),
            pltpu.VMEM((n * nr, 1, width), f32),
            pltpu.VMEM((1, 1, points), f32),
            pltpu.VMEM((max(nr - 1, 1), 1, points), f32),
            dma((3 + max(chunks, 2),)),
            dma((chunks,)),
            dma((chunks,)),
            dma((chunks,)),
            dma((chunks,)),
            dma((max(sides - 1, 1), chunks)),
            dma((max(sides - 1, 1), chunks)),
            dma(()),
            dma(()),
            dma((max(nr - 1, 1),)),
            dma((max(nr - 1, 1),)),
        ],
        compiler_params=pltpu.CompilerParams(collective_id=0, has_side_effects=True, vmem_limit_bytes=VMEM),
    )(src_green, rcv_green, model.reshape(1, points), observed)
    return image.reshape(points)


def solution(mesh):
    placed = (
        P(None, "grp", "pts"),
        P(None, ("grp", "rcv"), "pts"),
        P(("grp", "pts")),
        P(("grp", "pts"), None, "rcv"),
    )
    return jax.shard_map(
        local, mesh=mesh, in_specs=placed, out_specs=P(("grp", "pts")), check_vma=False
    )
```

```python
import functools
import math

import jax
import jax.numpy as jnp
from jax import lax
from jax.experimental import pallas as pl
from jax.experimental.pallas import tpu as pltpu
from jax.sharding import PartitionSpec as P

MESH = pl.DeviceIdType.MESH
UNROLL = 16
GROUP = 8
FINE = 4
VMEM = 56550500


def split(a):
    high = a.astype(jnp.bfloat16)
    low = (a - high.astype(jnp.float32)).astype(jnp.bfloat16)
    return high, low


def product(a, b_high, b_low, b_axis):
    rows = a.shape[0]
    a_high, a_low = split(a)
    dims = (((1,), (b_axis,)), ((), ()))
    both = lax.dot_general(
        jnp.concatenate([a_high, a_low], axis=0), b_high, dims, preferred_element_type=jnp.float32
    )
    cross = lax.dot_general(a_high, b_low, dims, preferred_element_type=jnp.float32)
    return both[:rows] + (both[rows:] + cross)


def kernel(
    n, nr, scale,
    src_hbm, rcv_hbm, model_hbm, obs_hbm, out_ref,
    src, rcv, model, obs, b_high, b_low, part, rbuf, zsend, zbuf, resid, gath, obst, told, ebuf, img, img_in,
    load, rs, rr, gs, gr, zs, zr, es, er, ims, imr,
):
    p = lax.axis_index("pts")
    c = lax.axis_index("rcv")
    sources = src.shape[1]
    receivers = rcv.shape[1]
    chunks, m, sides, _, block, width = part.shape
    side, place = p // m, p % m
    owner = nr - 1
    owns = c == owner
    behind = owner - c
    last = sides - 1
    tells = jnp.logical_and(owns, side == last)
    halves = max(chunks // 2, 1)
    per_half = chunks // halves
    half = per_half * width
    paired = m <= UNROLL and m & (m - 1) == 0
    group = GROUP // sides if m % (GROUP // sides) == 0 else 1
    rows = group * sides * block
    tiles = 2 * sides
    pieces = []
    for k in range(chunks):
        if k < FINE:
            pieces += [(k, pl.ds(t, 1)) for t in range(sides)]
        else:
            pieces.append((k, pl.ds(0, sides)))

    def peer(o):
        if not paired:
            return (place + o) % m
        q, bit = place, 1
        while bit < m:
            if o & bit:
                q = q + bit * (1 - 2 * ((place // bit) % 2))
            bit *= 2
        return q

    def origin(o):
        return peer(o) if paired else (place + m - o) % m

    def at_core(o, core):
        return {"pts": side * m + peer(o), "rcv": core}

    def each(start, stop, body):
        if stop - start <= UNROLL:
            for o in reversed(range(start, stop)):
                body(o)
        else:

            @pl.loop(start, stop)
            def _(o):
                body(o)

    loads = [
        pltpu.make_async_copy(src_hbm, src, load.at[0]),
        pltpu.make_async_copy(model_hbm, model, load.at[1]),
    ]
    for h in range(halves):
        for i in range(2):
            loads.append(pltpu.make_async_copy(
                rcv_hbm.at[i, pl.ds(h * half, half)], rcv.at[i, pl.ds(h * half, half)], load.at[3 + 2 * h + i]
            ))
    obs_load = pltpu.make_async_copy(obs_hbm, obs, load.at[2])
    for copy in loads[2:4] + loads[:2] + loads[4:]:
        copy.start()
    obs_load.start()

    barrier = pltpu.get_barrier_semaphore()
    partners = [((side + t) % sides) * m + place for t in range(1, sides)]

    def greet(device):
        pl.semaphore_signal(barrier, inc=1, device_id=device, device_id_type=MESH)

    def to_owner(o):
        greet(at_core(o, owner))

    each(1, m, to_owner)
    for d in range(1, nr):
        greet({"rcv": (c + d) % nr})

    @pl.when(owns)
    def _():
        for partner in partners:
            greet({"pts": partner})

        def to_others(o):
            for core in range(owner):
                greet(at_core(o, core))

        each(1, m, to_others)

    @pl.when(side != last)
    def _():
        def to_teller(o):
            greet({"pts": last * m + peer(o), "rcv": owner})

        each(1, m, to_teller)
        pl.when(jnp.logical_not(owns))(functools.partial(to_teller, 0))

    loads[0].wait()
    loads[1].wait()

    def rows_from(part_of, first, device):
        return jnp.concatenate(
            [
                src[part_of, pl.ds(pl.multiple_of((t * m + device(first + i)) * block, block), block)]
                for i in range(group)
                for t in range(sides)
            ],
            axis=0,
        )

    def sum_copy(i, o):
        k, at = pieces[i]
        return pltpu.make_async_remote_copy(
            part.at[k, o, at], rbuf.at[k, o * nr + behind, at], rs.at[i], rr.at[i],
            device_id=at_core(o, owner), device_id_type=MESH,
        )

    for h in range(halves):
        at = pl.ds(h * half, half)
        loads[2 + 2 * h].wait()
        b_high[0, at], b_low[0, at] = split(rcv[0, at])
        loads[3 + 2 * h].wait()
        b_high[1, at], b_low[1, at] = split(rcv[1, at])

        def forward(g):
            weight = model[...]
            scaled = jnp.concatenate(
                [rows_from(0, g * group, peer) * weight, rows_from(1, g * group, peer) * weight], axis=0
            )
            with_real = product(scaled, b_high[0, at], b_low[0, at], 1)
            with_imag = product(scaled, b_high[1, at], b_low[1, at], 1)
            real = (with_real[:rows] - with_imag[rows:]).reshape(group, sides, block, half)
            imag = (with_imag[:rows] + with_real[rows:]).reshape(group, sides, block, half)
            for j in range(per_half):
                k = h * per_half + j
                part[k, pl.ds(g * group, group), :, 0] = real[..., j * width:(j + 1) * width]
                part[k, pl.ds(g * group, group), :, 1] = imag[..., j * width:(j + 1) * width]

        each(0, m // group, forward)
        if h == 0:

            @pl.when(jnp.logical_and(owns, side != last))
            def _():
                pl.semaphore_wait(barrier, m * nr - 1 + len(partners))

            @pl.when(tells)
            def _():
                pl.semaphore_wait(barrier, sides * m * nr - 1)

            @pl.when(jnp.logical_not(owns))
            def _():
                pl.semaphore_wait(barrier, m - 1 + nr - 1)

            obs_load.wait()
            for t in range(sides):
                for i in range(2):
                    mine = jnp.where(side == t, obs[:, i, :], 0.0)
                    for k in range(chunks):
                        obst[k, t, i] = mine[:, k * width:(k + 1) * width]
        for j in range(per_half):
            k = h * per_half + j
            part[k, 0] = part[k, 0] - obst[k]
            for i, piece in enumerate(pieces):
                if piece[0] == k:
                    each(1, m, lambda o: sum_copy(i, o).start())
                    pl.when(jnp.logical_not(owns))(sum_copy(i, 0).start)

    def swap(i, t):
        k, at = pieces[i]
        return pltpu.make_async_remote_copy(
            zsend.at[k, at], zbuf.at[t, k, at], zs.at[t, i], zr.at[t, i],
            device_id={"pts": partners[t]}, device_id_type=MESH,
        )

    def residual_copy(k, o, core):
        return pltpu.make_async_remote_copy(
            resid.at[k, core], gath.at[k, o], gs.at[k], gr.at[k],
            device_id=at_core(o, core), device_id_type=MESH,
        )

    def spread(k):
        def to_peer(o):
            for core in range(nr):
                residual_copy(k, o, core).start()

        each(1, m, to_peer)
        for core in range(owner):
            residual_copy(k, 0, core).start()

    @pl.when(owns)
    def _():
        for i, (k, at) in enumerate(pieces):
            arrived = rbuf.at[k, pl.ds(1, m * nr - 1), at]
            pltpu.make_async_copy(arrived, arrived, rr.at[i]).wait()
            for core in range(nr):
                first = owner - core
                acc = part[k, 0, at] if core == owner else rbuf[k, first, at]
                if m <= UNROLL:
                    for o in range(1, m):
                        acc = acc + rbuf[k, o * nr + first, at]
                else:
                    acc = lax.fori_loop(1, m, lambda o, so_far: so_far + rbuf[k, o * nr + first, at], acc)
                zsend[k, at, core] = acc
            for t in range(len(partners)):
                swap(i, t).start()

        energy = jnp.zeros((block, width), jnp.float32)
        for k in range(chunks):
            for i, piece in enumerate(pieces):
                if piece[0] == k:
                    for t in range(len(partners)):
                        swap(i, t).wait_recv()
            for core in range(nr):
                whole = zsend[k, :, core]
                for t in range(len(partners)):
                    whole = whole + zbuf[t, k, :, core]
                whole = whole.reshape(tiles, block, width)
                resid[k, core] = whole
                energy = energy + jnp.sum(whole * whole, axis=0)
            gath[k, 0] = resid[k, owner]
            pl.when(side != last)(functools.partial(spread, k))
        energy = jnp.sum(energy, axis=0, keepdims=True)

        @pl.when(side == last)
        def _():
            told[0] = energy
            ebuf[0] = energy

            def tell(o, own=False):
                for t in range(sides):
                    for core in range(nr):
                        if not (own and t == last and core == owner):
                            pltpu.make_async_remote_copy(
                                told.at[0], ebuf.at[o], es, er,
                                device_id={"pts": t * m + peer(o), "rcv": core}, device_id_type=MESH,
                            ).start()

            each(1, m, tell)
            tell(0, own=True)
            for k in range(chunks):
                spread(k)

    def arrival(k, first):
        arrived = gath.at[k, pl.ds(first, m - first)]
        return pltpu.make_async_copy(arrived, arrived, gr.at[k])

    def energies(first):
        heard = ebuf.at[pl.ds(first, m - first)]
        return pltpu.make_async_copy(heard, heard, er)

    pl.when(tells)(energies(1).wait)
    pl.when(jnp.logical_not(tells))(energies(0).wait)
    summed = jnp.sum(jnp.sum(ebuf[pl.ds(0, m)], axis=0), axis=(0, 1), keepdims=True)
    spread_sq = summed / (sources * receivers * nr) + 1e-06
    inverse = 1.0 / spread_sq

    def gathered(g, h, part_of):
        return jnp.concatenate(
            [
                jnp.concatenate(
                    [
                        gath[k, g * group + i, 2 * t + part_of]
                        for i in range(group)
                        for t in range(sides)
                    ],
                    axis=0,
                )
                for k in range(h * per_half, (h + 1) * per_half)
            ],
            axis=1,
        )

    def image_of(g, h):
        at = pl.ds(h * half, half)
        real = gathered(g, h, 0)
        imag = gathered(g, h, 1)
        gain = 1.0 / (1.0 + (real * real + imag * imag) * inverse)
        weighted = jnp.concatenate([real * gain, imag * gain], axis=0)
        with_real = product(weighted, b_high[0, at], b_low[0, at], 0)
        with_imag = product(weighted, b_high[1, at], b_low[1, at], 0)
        back_real = with_real[:rows] + with_imag[rows:]
        back_imag = with_real[rows:] - with_imag[:rows]
        terms = rows_from(0, g * group, origin) * back_real + rows_from(1, g * group, origin) * back_imag
        return jnp.sum(terms, axis=0, keepdims=True)

    image = jnp.zeros((1, src.shape[2]), jnp.float32)
    for h in range(halves):
        for k in range(h * per_half, (h + 1) * per_half):
            pl.when(owns)(arrival(k, 1).wait)
            pl.when(jnp.logical_not(owns))(arrival(k, 0).wait)
        if m // group == 1:
            image = image + image_of(0, h)
        else:
            image = lax.fori_loop(0, m // group, lambda g, so_far: so_far + image_of(g, h), image)
    image = image * scale
    img[0] = image
    sums = []
    for d in range(1, nr):
        copy = pltpu.make_async_remote_copy(
            img.at[0], img_in.at[d - 1], ims.at[d - 1], imr.at[d - 1],
            device_id={"rcv": (c + d) % nr}, device_id_type=MESH,
        )
        copy.start()
        sums.append(copy)

    def sums_left(i, first):
        k, at = pieces[i]
        sent = part.at[k, pl.ds(first, m - first), at]
        return pltpu.make_async_copy(sent, sent, rs.at[i])

    def residuals_left(k):
        sent = gath.at[k, pl.ds(0, m * nr - 1)]
        return pltpu.make_async_copy(sent, sent, gs.at[k])

    for i in range(len(pieces)):
        pl.when(jnp.logical_not(owns))(sums_left(i, 0).wait)

    @pl.when(owns)
    def _():
        for i in range(len(pieces)):
            sums_left(i, 1).wait()
            for t in range(len(partners)):
                swap(i, t).wait_send()
        for k in range(chunks):
            residuals_left(k).wait()

    @pl.when(tells)
    def _():
        every = ebuf.at[pl.ds(0, n * nr - 1)]
        pltpu.make_async_copy(every, every, es).wait()

    for copy in sums:
        copy.wait_recv()
    for d in range(1, nr):
        image = image + img_in[d - 1]
    out_ref[...] = image
    for copy in sums:
        copy.wait_send()


def local(src_green, rcv_green, model, observed):
    n = lax.axis_size("pts")
    nr = lax.axis_size("rcv")
    sources, points = src_green.shape[1:]
    receivers = rcv_green.shape[1]
    block = observed.shape[0]
    scale = math.sqrt(points * n / (receivers * nr * sources))
    f32, bf16 = jnp.float32, jnp.bfloat16
    dma = pltpu.SemaphoreType.DMA
    width = 128 if receivers % 256 == 0 else receivers
    chunks = receivers // width
    sides = 2 if n % 2 == 0 and n > 2 else 1
    m = n // sides
    blocks = (sides, 2, block, width)
    tiles = (2 * sides, block, width)
    by_side = (chunks, sides, nr, 2, block, width)
    parts = chunks * sides
    image = pl.pallas_call(
        functools.partial(kernel, n, nr, scale),
        out_shape=jax.ShapeDtypeStruct((1, points), f32),
        in_specs=[pl.BlockSpec(memory_space=pl.ANY)] * 4,
        out_specs=pl.BlockSpec(memory_space=pltpu.VMEM),
        scratch_shapes=[
            pltpu.VMEM(src_green.shape, f32),
            pltpu.VMEM(rcv_green.shape, f32),
            pltpu.VMEM((1, points), f32),
            pltpu.VMEM(observed.shape, f32),
            pltpu.VMEM(rcv_green.shape, bf16),
            pltpu.VMEM(rcv_green.shape, bf16),
            pltpu.VMEM((chunks, m) + blocks, f32),
            pltpu.VMEM((chunks, m * nr) + blocks, f32),
            pltpu.VMEM(by_side, f32),
            pltpu.VMEM((max(sides - 1, 1),) + by_side, f32),
            pltpu.VMEM((chunks, nr) + tiles, f32),
            pltpu.VMEM((chunks, m * nr) + tiles, f32),
            pltpu.VMEM((chunks,) + blocks, f32),
            pltpu.VMEM((1, 1, width), f32),
            pltpu.VMEM((n * nr, 1, width), f32),
            pltpu.VMEM((1, 1, points), f32),
            pltpu.VMEM((max(nr - 1, 1), 1, points), f32),
            dma((3 + max(chunks, 2),)),
            dma((parts,)),
            dma((parts,)),
            dma((chunks,)),
            dma((chunks,)),
            dma((max(sides - 1, 1), parts)),
            dma((max(sides - 1, 1), parts)),
            dma(()),
            dma(()),
            dma((max(nr - 1, 1),)),
            dma((max(nr - 1, 1),)),
        ],
        compiler_params=pltpu.CompilerParams(collective_id=0, has_side_effects=True, vmem_limit_bytes=VMEM),
    )(src_green, rcv_green, model.reshape(1, points), observed)
    return image.reshape(points)


def solution(mesh):
    placed = (
        P(None, "grp", "pts"),
        P(None, ("grp", "rcv"), "pts"),
        P(("grp", "pts")),
        P(("grp", "pts"), None, "rcv"),
    )
    return jax.shard_map(
        local, mesh=mesh, in_specs=placed, out_specs=P(("grp", "pts")), check_vma=False
    )
```

```python
import functools
import math

import jax
import jax.numpy as jnp
from jax import lax
from jax.experimental import pallas as pl
from jax.experimental.pallas import tpu as pltpu
from jax.sharding import PartitionSpec as P

MESH = pl.DeviceIdType.MESH
UNROLL = 16
GROUP = 8
LAG = 1
VMEM = 56550500


def split(a):
    high = a.astype(jnp.bfloat16)
    low = (a - high.astype(jnp.float32)).astype(jnp.bfloat16)
    return high, low


def product(a, b_high, b_low, b_axis):
    rows = a.shape[0]
    a_high, a_low = split(a)
    dims = (((1,), (b_axis,)), ((), ()))
    both = lax.dot_general(
        jnp.concatenate([a_high, a_low], axis=0), b_high, dims, preferred_element_type=jnp.float32
    )
    cross = lax.dot_general(a_high, b_low, dims, preferred_element_type=jnp.float32)
    return both[:rows] + (both[rows:] + cross)


def kernel(
    n, nr, scale,
    src_hbm, rcv_hbm, model_hbm, obs_hbm, out_ref,
    src, rcv, model, obs, b_high, b_low, part, rbuf, zsend, zbuf, resid, gath, obst, told, ebuf, img, img_in,
    load, rs, rr, gs, gr, zs, zr, es, er, ims, imr,
):
    p = lax.axis_index("pts")
    c = lax.axis_index("rcv")
    sources = src.shape[1]
    receivers = rcv.shape[1]
    chunks, m, sides, _, block, width = part.shape
    side = p // m
    shift = m // 2 if sides == 2 and m % 2 == 0 else 0
    place = (p + side * shift) % m

    def device_at(t, lies):
        return t * m + (lies + t * shift) % m

    owner = nr - 1
    owns = c == owner
    behind = owner - c
    last = sides - 1
    tells = jnp.logical_and(owns, side == last)
    halves = max(chunks // 2, 1)
    per_half = chunks // halves
    half = per_half * width
    paired = m <= UNROLL and m & (m - 1) == 0
    group = GROUP // sides if m % (GROUP // sides) == 0 else 1
    rows = group * sides * block
    tiles = 2 * sides
    pieces = sorted(
        ((k, core) for k in range(chunks) for core in range(nr)),
        key=lambda piece: (piece[0] + LAG * (owner - piece[1]), piece[1]),
    )

    def peer(o):
        if not paired:
            return (place + o) % m
        q, bit = place, 1
        while bit < m:
            if o & bit:
                q = q + bit * (1 - 2 * ((place // bit) % 2))
            bit *= 2
        return q

    def origin(o):
        return peer(o) if paired else (place + m - o) % m

    def at_core(o, core):
        return {"pts": device_at(side, peer(o)), "rcv": core}

    def each(start, stop, body):
        if stop - start <= UNROLL:
            for o in reversed(range(start, stop)):
                body(o)
        else:

            @pl.loop(start, stop)
            def _(o):
                body(o)

    loads = [
        pltpu.make_async_copy(src_hbm, src, load.at[0]),
        pltpu.make_async_copy(model_hbm, model, load.at[1]),
    ]
    for h in range(halves):
        for i in range(2):
            loads.append(pltpu.make_async_copy(
                rcv_hbm.at[i, pl.ds(h * half, half)], rcv.at[i, pl.ds(h * half, half)], load.at[3 + 2 * h + i]
            ))
    obs_load = pltpu.make_async_copy(obs_hbm, obs, load.at[2])
    for copy in loads[2:4] + loads[:2] + loads[4:]:
        copy.start()
    obs_load.start()

    barrier = pltpu.get_barrier_semaphore()
    partners = [device_at((side + t) % sides, place) for t in range(1, sides)]

    def greet(device):
        pl.semaphore_signal(barrier, inc=1, device_id=device, device_id_type=MESH)

    def to_owner(o):
        greet(at_core(o, owner))

    each(1, m, to_owner)
    for d in range(1, nr):
        greet({"rcv": (c + d) % nr})

    @pl.when(owns)
    def _():
        for partner in partners:
            greet({"pts": partner})

        def to_others(o):
            for core in range(owner):
                greet(at_core(o, core))

        each(1, m, to_others)

    @pl.when(side != last)
    def _():
        def to_teller(o):
            greet({"pts": device_at(last, peer(o)), "rcv": owner})

        each(1, m, to_teller)
        pl.when(jnp.logical_not(owns))(functools.partial(to_teller, 0))

    loads[0].wait()
    loads[1].wait()

    def rows_from(part_of, first, device):
        return jnp.concatenate(
            [
                src[part_of, pl.ds(pl.multiple_of(device_at(t, device(first + i)) * block, block), block)]
                for i in range(group)
                for t in range(sides)
            ],
            axis=0,
        )

    def sum_copy(k, o):
        return pltpu.make_async_remote_copy(
            part.at[k, o], rbuf.at[k, behind, o], rs.at[k], rr.at[k, behind],
            device_id=at_core(o, owner), device_id_type=MESH,
        )

    for h in range(halves):
        at = pl.ds(h * half, half)
        loads[2 + 2 * h].wait()
        b_high[0, at], b_low[0, at] = split(rcv[0, at])
        loads[3 + 2 * h].wait()
        b_high[1, at], b_low[1, at] = split(rcv[1, at])

        def forward(g):
            weight = model[...]
            scaled = jnp.concatenate(
                [rows_from(0, g * group, peer) * weight, rows_from(1, g * group, peer) * weight], axis=0
            )
            with_real = product(scaled, b_high[0, at], b_low[0, at], 1)
            with_imag = product(scaled, b_high[1, at], b_low[1, at], 1)
            real = (with_real[:rows] - with_imag[rows:]).reshape(group, sides, block, half)
            imag = (with_imag[:rows] + with_real[rows:]).reshape(group, sides, block, half)
            for j in range(per_half):
                k = h * per_half + j
                part[k, pl.ds(g * group, group), :, 0] = real[..., j * width:(j + 1) * width]
                part[k, pl.ds(g * group, group), :, 1] = imag[..., j * width:(j + 1) * width]

        each(0, m // group, forward)
        if h == 0:

            @pl.when(jnp.logical_and(owns, side != last))
            def _():
                pl.semaphore_wait(barrier, m * nr - 1 + len(partners))

            @pl.when(tells)
            def _():
                pl.semaphore_wait(barrier, sides * m * nr - 1)

            @pl.when(jnp.logical_not(owns))
            def _():
                pl.semaphore_wait(barrier, m - 1 + nr - 1)

            obs_load.wait()
            for t in range(sides):
                for i in range(2):
                    mine = jnp.where(side == t, obs[:, i, :], 0.0)
                    for k in range(chunks):
                        obst[k, t, i] = mine[:, k * width:(k + 1) * width]
        for j in range(per_half):
            k = h * per_half + j
            each(1, m, lambda o: sum_copy(k, o).start())
            part[k, 0] = part[k, 0] - obst[k]
            pl.when(jnp.logical_not(owns))(sum_copy(k, 0).start)

    def swap(k, core, t):
        return pltpu.make_async_remote_copy(
            zsend.at[k, core], zbuf.at[t, k, core], zs.at[t, k, core], zr.at[t, k, core],
            device_id={"pts": partners[t]}, device_id_type=MESH,
        )

    def residual_copy(k, o, core):
        return pltpu.make_async_remote_copy(
            resid.at[k, core], gath.at[k, o], gs.at[k], gr.at[k],
            device_id=at_core(o, core), device_id_type=MESH,
        )

    def spread(k, core):
        each(1, m, lambda o: residual_copy(k, o, core).start())
        if core != owner:
            residual_copy(k, 0, core).start()

    @pl.when(owns)
    def _():
        for k, core in pieces:
            back = owner - core
            first = 0 if back else 1
            arrived = rbuf.at[k, back, pl.ds(first, m - first)]
            pltpu.make_async_copy(arrived, arrived, rr.at[k, back]).wait()
            acc = rbuf[k, back, 0] if back else part[k, 0]
            if m <= UNROLL:
                for o in range(1, m):
                    acc = acc + rbuf[k, back, o]
            else:
                acc = lax.fori_loop(1, m, lambda o, so_far: so_far + rbuf[k, back, o], acc)
            zsend[k, core] = acc
            for t in range(len(partners)):
                swap(k, core, t).start()

        energy = jnp.zeros((block, width), jnp.float32)
        for k, core in pieces:
            whole = zsend[k, core]
            for t in range(len(partners)):
                swap(k, core, t).wait_recv()
                whole = whole + zbuf[t, k, core]
            whole = whole.reshape(tiles, block, width)
            resid[k, core] = whole
            energy = energy + jnp.sum(whole * whole, axis=0)
            if core == owner:
                gath[k, 0] = whole
            pl.when(side != last)(functools.partial(spread, k, core))
        energy = jnp.sum(energy, axis=0, keepdims=True)

        @pl.when(side == last)
        def _():
            told[0] = energy
            ebuf[0] = energy

            def tell(o, own=False):
                for t in range(sides):
                    for core in range(nr):
                        if not (own and t == last and core == owner):
                            pltpu.make_async_remote_copy(
                                told.at[0], ebuf.at[o], es, er,
                                device_id={"pts": device_at(t, peer(o)), "rcv": core}, device_id_type=MESH,
                            ).start()

            each(1, m, tell)
            tell(0, own=True)
            for k, core in pieces:
                spread(k, core)

    def arrival(k, first):
        arrived = gath.at[k, pl.ds(first, m - first)]
        return pltpu.make_async_copy(arrived, arrived, gr.at[k])

    def energies(first):
        heard = ebuf.at[pl.ds(first, m - first)]
        return pltpu.make_async_copy(heard, heard, er)

    pl.when(tells)(energies(1).wait)
    pl.when(jnp.logical_not(tells))(energies(0).wait)
    summed = jnp.sum(jnp.sum(ebuf[pl.ds(0, m)], axis=0), axis=(0, 1), keepdims=True)
    spread_sq = summed / (sources * receivers * nr) + 1e-06
    inverse = 1.0 / spread_sq

    def gathered(g, h, part_of):
        return jnp.concatenate(
            [
                jnp.concatenate(
                    [
                        gath[k, g * group + i, 2 * t + part_of]
                        for i in range(group)
                        for t in range(sides)
                    ],
                    axis=0,
                )
                for k in range(h * per_half, (h + 1) * per_half)
            ],
            axis=1,
        )

    def image_of(g, h):
        at = pl.ds(h * half, half)
        real = gathered(g, h, 0)
        imag = gathered(g, h, 1)
        gain = 1.0 / (1.0 + (real * real + imag * imag) * inverse)
        weighted = jnp.concatenate([real * gain, imag * gain], axis=0)
        with_real = product(weighted, b_high[0, at], b_low[0, at], 0)
        with_imag = product(weighted, b_high[1, at], b_low[1, at], 0)
        back_real = with_real[:rows] + with_imag[rows:]
        back_imag = with_real[rows:] - with_imag[:rows]
        terms = rows_from(0, g * group, origin) * back_real + rows_from(1, g * group, origin) * back_imag
        return jnp.sum(terms, axis=0, keepdims=True)

    image = jnp.zeros((1, src.shape[2]), jnp.float32)
    for h in range(halves):
        for k in range(h * per_half, (h + 1) * per_half):
            pl.when(owns)(arrival(k, 1).wait)
            pl.when(jnp.logical_not(owns))(arrival(k, 0).wait)
        if m // group == 1:
            image = image + image_of(0, h)
        else:
            image = lax.fori_loop(0, m // group, lambda g, so_far: so_far + image_of(g, h), image)
    image = image * scale
    img[0] = image
    sums = []
    for d in range(1, nr):
        copy = pltpu.make_async_remote_copy(
            img.at[0], img_in.at[d - 1], ims.at[d - 1], imr.at[d - 1],
            device_id={"rcv": (c + d) % nr}, device_id_type=MESH,
        )
        copy.start()
        sums.append(copy)

    def sums_left(k, first):
        sent = part.at[k, pl.ds(first, m - first)]
        return pltpu.make_async_copy(sent, sent, rs.at[k])

    def residuals_left(k):
        sent = gath.at[k, pl.ds(0, m * nr - 1)]
        return pltpu.make_async_copy(sent, sent, gs.at[k])

    for k in range(chunks):
        pl.when(jnp.logical_not(owns))(sums_left(k, 0).wait)

    @pl.when(owns)
    def _():
        for k in range(chunks):
            sums_left(k, 1).wait()
            for core in range(nr):
                for t in range(len(partners)):
                    swap(k, core, t).wait_send()
            residuals_left(k).wait()

    @pl.when(tells)
    def _():
        every = ebuf.at[pl.ds(0, n * nr - 1)]
        pltpu.make_async_copy(every, every, es).wait()

    for copy in sums:
        copy.wait_recv()
    for d in range(1, nr):
        image = image + img_in[d - 1]
    out_ref[...] = image
    for copy in sums:
        copy.wait_send()


def local(src_green, rcv_green, model, observed):
    n = lax.axis_size("pts")
    nr = lax.axis_size("rcv")
    sources, points = src_green.shape[1:]
    receivers = rcv_green.shape[1]
    block = observed.shape[0]
    scale = math.sqrt(points * n / (receivers * nr * sources))
    f32, bf16 = jnp.float32, jnp.bfloat16
    dma = pltpu.SemaphoreType.DMA
    width = 128 if receivers % 256 == 0 else receivers
    chunks = receivers // width
    sides = 2 if n % 2 == 0 and n > 2 else 1
    m = n // sides
    blocks = (sides, 2, block, width)
    tiles = (2 * sides, block, width)
    image = pl.pallas_call(
        functools.partial(kernel, n, nr, scale),
        out_shape=jax.ShapeDtypeStruct((1, points), f32),
        in_specs=[pl.BlockSpec(memory_space=pl.ANY)] * 4,
        out_specs=pl.BlockSpec(memory_space=pltpu.VMEM),
        scratch_shapes=[
            pltpu.VMEM(src_green.shape, f32),
            pltpu.VMEM(rcv_green.shape, f32),
            pltpu.VMEM((1, points), f32),
            pltpu.VMEM(observed.shape, f32),
            pltpu.VMEM(rcv_green.shape, bf16),
            pltpu.VMEM(rcv_green.shape, bf16),
            pltpu.VMEM((chunks, m) + blocks, f32),
            pltpu.VMEM((chunks, nr, m) + blocks, f32),
            pltpu.VMEM((chunks, nr) + blocks, f32),
            pltpu.VMEM((max(sides - 1, 1), chunks, nr) + blocks, f32),
            pltpu.VMEM((chunks, nr) + tiles, f32),
            pltpu.VMEM((chunks, m * nr) + tiles, f32),
            pltpu.VMEM((chunks,) + blocks, f32),
            pltpu.VMEM((1, 1, width), f32),
            pltpu.VMEM((n * nr, 1, width), f32),
            pltpu.VMEM((1, 1, points), f32),
            pltpu.VMEM((max(nr - 1, 1), 1, points), f32),
            dma((3 + max(chunks, 2),)),
            dma((chunks,)),
            dma((chunks, nr)),
            dma((chunks,)),
            dma((chunks,)),
            dma((max(sides - 1, 1), chunks, nr)),
            dma((max(sides - 1, 1), chunks, nr)),
            dma(()),
            dma(()),
            dma((max(nr - 1, 1),)),
            dma((max(nr - 1, 1),)),
        ],
        compiler_params=pltpu.CompilerParams(collective_id=0, has_side_effects=True, vmem_limit_bytes=VMEM),
    )(src_green, rcv_green, model.reshape(1, points), observed)
    return image.reshape(points)


def solution(mesh):
    placed = (
        P(None, "grp", "pts"),
        P(None, ("grp", "rcv"), "pts"),
        P(("grp", "pts")),
        P(("grp", "pts"), None, "rcv"),
    )
    return jax.shard_map(
        local, mesh=mesh, in_specs=placed, out_specs=P(("grp", "pts")), check_vma=False
    )
```

```python
import functools
import math

import jax
import jax.numpy as jnp
from jax import lax
from jax.experimental import pallas as pl
from jax.experimental.pallas import tpu as pltpu
from jax.sharding import PartitionSpec as P

MESH = pl.DeviceIdType.MESH
UNROLL = 16
GROUP = 8
LAG = 1
VMEM = 56550500


def split(a):
    high = a.astype(jnp.bfloat16)
    low = (a - high.astype(jnp.float32)).astype(jnp.bfloat16)
    return high, low


def product(a, b_high, b_low, b_axis):
    rows = a.shape[0]
    a_high, a_low = split(a)
    dims = (((1,), (b_axis,)), ((), ()))
    both = lax.dot_general(
        jnp.concatenate([a_high, a_low], axis=0), b_high, dims, preferred_element_type=jnp.float32
    )
    cross = lax.dot_general(a_high, b_low, dims, preferred_element_type=jnp.float32)
    return both[:rows] + (both[rows:] + cross)


def kernel(
    n, nr, scale,
    src_hbm, rcv_hbm, model_hbm, obs_hbm, out_ref,
    src, rcv, model, obs, b_high, b_low, part, rbuf, zsend, zbuf, resid, gath, obst, told, ebuf, img, img_in,
    load, rs, rr, gs, gr, zs, zr, es, er, ims, imr,
):
    p = lax.axis_index("pts")
    c = lax.axis_index("rcv")
    sources = src.shape[1]
    receivers = rcv.shape[1]
    chunks, m, sides, _, block, width = part.shape
    side = p // m
    shift = m // 2 if sides == 2 and m % 2 == 0 else 0
    place = (p + side * shift) % m

    def device_at(t, lies):
        return t * m + (lies + t * shift) % m

    owner = nr - 1
    owns = c == owner
    behind = owner - c
    last = sides - 1
    tells = jnp.logical_and(owns, side == last)
    halves = max(chunks // 2, 1)
    per_half = chunks // halves
    half = per_half * width
    paired = m <= UNROLL and m & (m - 1) == 0
    group = GROUP // sides if m % (GROUP // sides) == 0 else 1
    rows = group * sides * block
    tiles = 2 * sides
    pieces = sorted(
        ((k, core) for k in range(chunks) for core in range(nr)),
        key=lambda piece: (piece[0] + LAG * (owner - piece[1]), piece[1]),
    )

    def peer(o):
        if not paired:
            return (place + o) % m
        q, bit = place, 1
        while bit < m:
            if o & bit:
                q = q + bit * (1 - 2 * ((place // bit) % 2))
            bit *= 2
        return q

    def origin(o):
        return peer(o) if paired else (place + m - o) % m

    def at_core(o, core):
        return {"pts": device_at(side, peer(o)), "rcv": core}

    def each(start, stop, body):
        if stop - start <= UNROLL:
            for o in reversed(range(start, stop)):
                body(o)
        else:

            @pl.loop(start, stop)
            def _(o):
                body(o)

    loads = [
        pltpu.make_async_copy(src_hbm, src, load.at[0]),
        pltpu.make_async_copy(model_hbm, model, load.at[1]),
    ]
    for h in range(halves):
        for i in range(2):
            loads.append(pltpu.make_async_copy(
                rcv_hbm.at[i, pl.ds(h * half, half)], rcv.at[i, pl.ds(h * half, half)], load.at[3 + 2 * h + i]
            ))
    obs_load = pltpu.make_async_copy(obs_hbm, obs, load.at[2])
    for copy in loads[2:4] + loads[:2] + loads[4:]:
        copy.start()
    obs_load.start()

    barrier = pltpu.get_barrier_semaphore()
    partners = [device_at((side + t) % sides, place) for t in range(1, sides)]

    def greet(device):
        pl.semaphore_signal(barrier, inc=1, device_id=device, device_id_type=MESH)

    def to_owner(o):
        greet(at_core(o, owner))

    each(1, m, to_owner)
    for d in range(1, nr):
        greet({"rcv": (c + d) % nr})

    @pl.when(owns)
    def _():
        for partner in partners:
            greet({"pts": partner})

        def to_others(o):
            for core in range(owner):
                greet(at_core(o, core))

        each(1, m, to_others)

    @pl.when(side != last)
    def _():
        def to_teller(o):
            greet({"pts": device_at(last, peer(o)), "rcv": owner})

        each(1, m, to_teller)
        pl.when(jnp.logical_not(owns))(functools.partial(to_teller, 0))

    loads[0].wait()
    loads[1].wait()

    def rows_from(part_of, first, device):
        return jnp.concatenate(
            [
                src[part_of, pl.ds(pl.multiple_of(device_at(t, device(first + i)) * block, block), block)]
                for i in range(group)
                for t in range(sides)
            ],
            axis=0,
        )

    def sum_copy(k, o):
        return pltpu.make_async_remote_copy(
            part.at[k, o], rbuf.at[k, behind, o], rs.at[k], rr.at[k, behind],
            device_id=at_core(o, owner), device_id_type=MESH,
        )

    for h in range(halves):
        at = pl.ds(h * half, half)
        loads[2 + 2 * h].wait()
        b_high[0, at], b_low[0, at] = split(rcv[0, at])
        loads[3 + 2 * h].wait()
        b_high[1, at], b_low[1, at] = split(rcv[1, at])

        def forward(g):
            weight = model[...]
            scaled = jnp.concatenate(
                [rows_from(0, g * group, peer) * weight, rows_from(1, g * group, peer) * weight], axis=0
            )
            with_real = product(scaled, b_high[0, at], b_low[0, at], 1)
            with_imag = product(scaled, b_high[1, at], b_low[1, at], 1)
            real = (with_real[:rows] - with_imag[rows:]).reshape(group, sides, block, half)
            imag = (with_imag[:rows] + with_real[rows:]).reshape(group, sides, block, half)
            for j in range(per_half):
                k = h * per_half + j
                part[k, pl.ds(g * group, group), :, 0] = real[..., j * width:(j + 1) * width]
                part[k, pl.ds(g * group, group), :, 1] = imag[..., j * width:(j + 1) * width]

        each(0, m // group, forward)
        if h == 0:

            @pl.when(jnp.logical_and(owns, side != last))
            def _():
                pl.semaphore_wait(barrier, m * nr - 1 + len(partners))

            @pl.when(tells)
            def _():
                pl.semaphore_wait(barrier, sides * m * nr - 1)

            @pl.when(jnp.logical_not(owns))
            def _():
                pl.semaphore_wait(barrier, m - 1 + nr - 1)

            obs_load.wait()
            for t in range(sides):
                for i in range(2):
                    mine = jnp.where(side == t, obs[:, i, :], 0.0)
                    for k in range(chunks):
                        obst[k, t, i] = mine[:, k * width:(k + 1) * width]
        for j in range(per_half):
            k = h * per_half + j
            each(1, m, lambda o: sum_copy(k, o).start())
            part[k, 0] = part[k, 0] - obst[k]
            pl.when(jnp.logical_not(owns))(sum_copy(k, 0).start)

    def swap(k, core, t):
        return pltpu.make_async_remote_copy(
            zsend.at[k, core], zbuf.at[t, k, core], zs.at[t, k, core], zr.at[t, k, core],
            device_id={"pts": partners[t]}, device_id_type=MESH,
        )

    def residual_copy(k, o, core):
        return pltpu.make_async_remote_copy(
            resid.at[k, core], gath.at[k, o], gs.at[k], gr.at[k],
            device_id=at_core(o, core), device_id_type=MESH,
        )

    def spread(k, core):
        each(1, m, lambda o: residual_copy(k, o, core).start())
        if core != owner:
            residual_copy(k, 0, core).start()

    @pl.when(owns)
    def _():
        for k, core in pieces:
            back = owner - core
            first = 0 if back else 1
            arrived = rbuf.at[k, back, pl.ds(first, m - first)]
            pltpu.make_async_copy(arrived, arrived, rr.at[k, back]).wait()
            acc = rbuf[k, back, 0] if back else part[k, 0]
            if m <= UNROLL:
                for o in range(1, m):
                    acc = acc + rbuf[k, back, o]
            else:
                acc = lax.fori_loop(1, m, lambda o, so_far: so_far + rbuf[k, back, o], acc)
            zsend[k, core] = acc
            for t in range(len(partners)):
                swap(k, core, t).start()

        energy = jnp.zeros((block, width), jnp.float32)
        for k, core in pieces:
            whole = zsend[k, core]
            for t in range(len(partners)):
                swap(k, core, t).wait_recv()
                whole = whole + zbuf[t, k, core]
            whole = whole.reshape(tiles, block, width)
            resid[k, core] = whole
            pl.when(side != last)(functools.partial(spread, k, core))
            energy = energy + jnp.sum(whole * whole, axis=0)
            if core == owner:
                gath[k, 0] = whole
        energy = jnp.sum(energy, axis=0, keepdims=True)

        @pl.when(side == last)
        def _():
            told[0] = energy
            ebuf[0] = energy

            def tell(o, own=False):
                for t in range(sides):
                    for core in range(nr):
                        if not (own and t == last and core == owner):
                            pltpu.make_async_remote_copy(
                                told.at[0], ebuf.at[o], es, er,
                                device_id={"pts": device_at(t, peer(o)), "rcv": core}, device_id_type=MESH,
                            ).start()

            each(1, m, tell)
            tell(0, own=True)
            for k, core in pieces:
                spread(k, core)

    def arrival(k, first):
        arrived = gath.at[k, pl.ds(first, m - first)]
        return pltpu.make_async_copy(arrived, arrived, gr.at[k])

    def energies(first):
        heard = ebuf.at[pl.ds(first, m - first)]
        return pltpu.make_async_copy(heard, heard, er)

    pl.when(tells)(energies(1).wait)
    pl.when(jnp.logical_not(tells))(energies(0).wait)
    summed = jnp.sum(jnp.sum(ebuf[pl.ds(0, m)], axis=0), axis=(0, 1), keepdims=True)
    spread_sq = summed / (sources * receivers * nr) + 1e-06
    inverse = 1.0 / spread_sq

    def gathered(g, h, part_of):
        return jnp.concatenate(
            [
                jnp.concatenate(
                    [
                        gath[k, g * group + i, 2 * t + part_of]
                        for i in range(group)
                        for t in range(sides)
                    ],
                    axis=0,
                )
                for k in range(h * per_half, (h + 1) * per_half)
            ],
            axis=1,
        )

    def image_of(g, h):
        at = pl.ds(h * half, half)
        real = gathered(g, h, 0)
        imag = gathered(g, h, 1)
        gain = 1.0 / (1.0 + (real * real + imag * imag) * inverse)
        weighted = jnp.concatenate([real * gain, imag * gain], axis=0)
        with_real = product(weighted, b_high[0, at], b_low[0, at], 0)
        with_imag = product(weighted, b_high[1, at], b_low[1, at], 0)
        back_real = with_real[:rows] + with_imag[rows:]
        back_imag = with_real[rows:] - with_imag[:rows]
        terms = rows_from(0, g * group, origin) * back_real + rows_from(1, g * group, origin) * back_imag
        return jnp.sum(terms, axis=0, keepdims=True)

    image = jnp.zeros((1, src.shape[2]), jnp.float32)
    for h in range(halves):
        for k in range(h * per_half, (h + 1) * per_half):
            pl.when(owns)(arrival(k, 1).wait)
            pl.when(jnp.logical_not(owns))(arrival(k, 0).wait)
        if m // group == 1:
            image = image + image_of(0, h)
        else:
            image = lax.fori_loop(0, m // group, lambda g, so_far: so_far + image_of(g, h), image)
    image = image * scale
    img[0] = image
    sums = []
    for d in range(1, nr):
        copy = pltpu.make_async_remote_copy(
            img.at[0], img_in.at[d - 1], ims.at[d - 1], imr.at[d - 1],
            device_id={"rcv": (c + d) % nr}, device_id_type=MESH,
        )
        copy.start()
        sums.append(copy)

    def sums_left(k, first):
        sent = part.at[k, pl.ds(first, m - first)]
        return pltpu.make_async_copy(sent, sent, rs.at[k])

    def residuals_left(k):
        sent = gath.at[k, pl.ds(0, m * nr - 1)]
        return pltpu.make_async_copy(sent, sent, gs.at[k])

    for k in range(chunks):
        pl.when(jnp.logical_not(owns))(sums_left(k, 0).wait)

    @pl.when(owns)
    def _():
        for k in range(chunks):
            sums_left(k, 1).wait()
            for core in range(nr):
                for t in range(len(partners)):
                    swap(k, core, t).wait_send()
            residuals_left(k).wait()

    @pl.when(tells)
    def _():
        every = ebuf.at[pl.ds(0, n * nr - 1)]
        pltpu.make_async_copy(every, every, es).wait()

    for copy in sums:
        copy.wait_recv()
    for d in range(1, nr):
        image = image + img_in[d - 1]
    out_ref[...] = image
    for copy in sums:
        copy.wait_send()


def local(src_green, rcv_green, model, observed):
    n = lax.axis_size("pts")
    nr = lax.axis_size("rcv")
    sources, points = src_green.shape[1:]
    receivers = rcv_green.shape[1]
    block = observed.shape[0]
    scale = math.sqrt(points * n / (receivers * nr * sources))
    f32, bf16 = jnp.float32, jnp.bfloat16
    dma = pltpu.SemaphoreType.DMA
    width = 128 if receivers % 256 == 0 else receivers
    chunks = receivers // width
    sides = 2 if n % 2 == 0 and n > 2 else 1
    m = n // sides
    blocks = (sides, 2, block, width)
    tiles = (2 * sides, block, width)
    image = pl.pallas_call(
        functools.partial(kernel, n, nr, scale),
        out_shape=jax.ShapeDtypeStruct((1, points), f32),
        in_specs=[pl.BlockSpec(memory_space=pl.ANY)] * 4,
        out_specs=pl.BlockSpec(memory_space=pltpu.VMEM),
        scratch_shapes=[
            pltpu.VMEM(src_green.shape, f32),
            pltpu.VMEM(rcv_green.shape, f32),
            pltpu.VMEM((1, points), f32),
            pltpu.VMEM(observed.shape, f32),
            pltpu.VMEM(rcv_green.shape, bf16),
            pltpu.VMEM(rcv_green.shape, bf16),
            pltpu.VMEM((chunks, m) + blocks, f32),
            pltpu.VMEM((chunks, nr, m) + blocks, f32),
            pltpu.VMEM((chunks, nr) + blocks, f32),
            pltpu.VMEM((max(sides - 1, 1), chunks, nr) + blocks, f32),
            pltpu.VMEM((chunks, nr) + tiles, f32),
            pltpu.VMEM((chunks, m * nr) + tiles, f32),
            pltpu.VMEM((chunks,) + blocks, f32),
            pltpu.VMEM((1, 1, width), f32),
            pltpu.VMEM((n * nr, 1, width), f32),
            pltpu.VMEM((1, 1, points), f32),
            pltpu.VMEM((max(nr - 1, 1), 1, points), f32),
            dma((3 + max(chunks, 2),)),
            dma((chunks,)),
            dma((chunks, nr)),
            dma((chunks,)),
            dma((chunks,)),
            dma((max(sides - 1, 1), chunks, nr)),
            dma((max(sides - 1, 1), chunks, nr)),
            dma(()),
            dma(()),
            dma((max(nr - 1, 1),)),
            dma((max(nr - 1, 1),)),
        ],
        compiler_params=pltpu.CompilerParams(collective_id=0, has_side_effects=True, vmem_limit_bytes=VMEM),
    )(src_green, rcv_green, model.reshape(1, points), observed)
    return image.reshape(points)


def solution(mesh):
    placed = (
        P(None, "grp", "pts"),
        P(None, ("grp", "rcv"), "pts"),
        P(("grp", "pts")),
        P(("grp", "pts"), None, "rcv"),
    )
    return jax.shard_map(
        local, mesh=mesh, in_specs=placed, out_specs=P(("grp", "pts")), check_vma=False
    )
```

```python
import functools
import math

import jax
import jax.numpy as jnp
from jax import lax
from jax.experimental import pallas as pl
from jax.experimental.pallas import tpu as pltpu
from jax.sharding import PartitionSpec as P

MESH = pl.DeviceIdType.MESH
UNROLL = 16
GROUP = 8
LAG = 1
VMEM = 56550500


def split(a):
    high = a.astype(jnp.bfloat16)
    low = (a - high.astype(jnp.float32)).astype(jnp.bfloat16)
    return high, low


def product(a, b_high, b_low, b_axis):
    rows = a.shape[0]
    a_high, a_low = split(a)
    dims = (((1,), (b_axis,)), ((), ()))
    both = lax.dot_general(
        jnp.concatenate([a_high, a_low], axis=0), b_high, dims, preferred_element_type=jnp.float32
    )
    cross = lax.dot_general(a_high, b_low, dims, preferred_element_type=jnp.float32)
    return both[:rows] + (both[rows:] + cross)


def kernel(
    n, nr, scale,
    src_hbm, rcv_hbm, model_hbm, obs_hbm, out_ref,
    src, rcv, model, obs, b_high, b_low, part, rbuf, zsend, zbuf, resid, gath, obst, told, ebuf, img, img_in,
    load, rs, rr, gs, gr, zs, zr, es, er, ims, imr,
):
    p = lax.axis_index("pts")
    c = lax.axis_index("rcv")
    sources = src.shape[1]
    receivers = rcv.shape[1]
    chunks, m, sides, _, block, width = part.shape
    side = p // m
    shift = m // 2 if sides == 2 and m % 2 == 0 else 0
    place = (p + side * shift) % m

    def device_at(t, lies):
        return t * m + (lies + t * shift) % m

    owner = nr - 1
    owns = c == owner
    behind = owner - c
    last = sides - 1
    tells = jnp.logical_and(owns, side == last)
    halves = max(chunks // 2, 1)
    per_half = chunks // halves
    half = per_half * width
    paired = m <= UNROLL and m & (m - 1) == 0
    group = GROUP // sides if m % (GROUP // sides) == 0 else 1
    rows = group * sides * block
    tiles = 2 * sides
    pieces = sorted(
        ((k, core) for k in range(chunks) for core in range(nr)),
        key=lambda piece: (piece[0] + LAG * (owner - piece[1]), piece[1]),
    )

    def peer(o):
        if not paired:
            return (place + o) % m
        q, bit = place, 1
        while bit < m:
            if o & bit:
                q = q + bit * (1 - 2 * ((place // bit) % 2))
            bit *= 2
        return q

    def origin(o):
        return peer(o) if paired else (place + m - o) % m

    def at_core(o, core):
        return {"pts": device_at(side, peer(o)), "rcv": core}

    def each(start, stop, body):
        if stop - start <= UNROLL:
            for o in reversed(range(start, stop)):
                body(o)
        else:

            @pl.loop(start, stop)
            def _(o):
                body(o)

    loads = [
        pltpu.make_async_copy(src_hbm, src, load.at[0]),
        pltpu.make_async_copy(model_hbm, model, load.at[1]),
    ]
    for h in range(halves):
        for i in range(2):
            loads.append(pltpu.make_async_copy(
                rcv_hbm.at[i, pl.ds(h * half, half)], rcv.at[i, pl.ds(h * half, half)], load.at[3 + 2 * h + i]
            ))
    obs_load = pltpu.make_async_copy(obs_hbm, obs, load.at[2])
    for copy in loads[2:4] + loads[:2] + loads[4:]:
        copy.start()
    obs_load.start()

    barrier = pltpu.get_barrier_semaphore()
    partners = [device_at((side + t) % sides, place) for t in range(1, sides)]

    def greet(device):
        pl.semaphore_signal(barrier, inc=1, device_id=device, device_id_type=MESH)

    def to_owner(o):
        greet(at_core(o, owner))

    each(1, m, to_owner)
    for d in range(1, nr):
        greet({"rcv": (c + d) % nr})

    @pl.when(owns)
    def _():
        for partner in partners:
            greet({"pts": partner})

        def to_others(o):
            for core in range(owner):
                greet(at_core(o, core))

        each(1, m, to_others)

    @pl.when(side != last)
    def _():
        def to_teller(o):
            greet({"pts": device_at(last, peer(o)), "rcv": owner})

        each(1, m, to_teller)
        pl.when(jnp.logical_not(owns))(functools.partial(to_teller, 0))

    loads[0].wait()
    loads[1].wait()

    def rows_from(part_of, first, device):
        return jnp.concatenate(
            [
                src[part_of, pl.ds(pl.multiple_of(device_at(t, device(first + i)) * block, block), block)]
                for i in range(group)
                for t in range(sides)
            ],
            axis=0,
        )

    def sum_copy(k, o):
        return pltpu.make_async_remote_copy(
            part.at[k, o], rbuf.at[k, behind, o], rs.at[k], rr.at[k, behind],
            device_id=at_core(o, owner), device_id_type=MESH,
        )

    for h in range(halves):
        at = pl.ds(h * half, half)
        loads[2 + 2 * h].wait()
        b_high[0, at], b_low[0, at] = split(rcv[0, at])
        loads[3 + 2 * h].wait()
        b_high[1, at], b_low[1, at] = split(rcv[1, at])

        def forward(g):
            weight = model[...]
            scaled = jnp.concatenate(
                [rows_from(0, g * group, peer) * weight, rows_from(1, g * group, peer) * weight], axis=0
            )
            with_real = product(scaled, b_high[0, at], b_low[0, at], 1)
            with_imag = product(scaled, b_high[1, at], b_low[1, at], 1)
            real = (with_real[:rows] - with_imag[rows:]).reshape(group, sides, block, half)
            imag = (with_imag[:rows] + with_real[rows:]).reshape(group, sides, block, half)
            for j in range(per_half):
                k = h * per_half + j
                part[k, pl.ds(g * group, group), :, 0] = real[..., j * width:(j + 1) * width]
                part[k, pl.ds(g * group, group), :, 1] = imag[..., j * width:(j + 1) * width]

        each(0, m // group, forward)
        if h == 0:

            @pl.when(jnp.logical_and(owns, side != last))
            def _():
                pl.semaphore_wait(barrier, m * nr - 1 + len(partners))

            @pl.when(tells)
            def _():
                pl.semaphore_wait(barrier, sides * m * nr - 1)

            @pl.when(jnp.logical_not(owns))
            def _():
                pl.semaphore_wait(barrier, m - 1 + nr - 1)

        for j in range(per_half):
            k = h * per_half + j
            each(1, m, lambda o: sum_copy(k, o).start())
        if h == 0:
            obs_load.wait()
            for t in range(sides):
                for i in range(2):
                    mine = jnp.where(side == t, obs[:, i, :], 0.0)
                    for k in range(chunks):
                        obst[k, t, i] = mine[:, k * width:(k + 1) * width]
        for j in range(per_half):
            k = h * per_half + j
            part[k, 0] = part[k, 0] - obst[k]
            pl.when(jnp.logical_not(owns))(sum_copy(k, 0).start)

    def swap(k, core, t):
        return pltpu.make_async_remote_copy(
            zsend.at[k, core], zbuf.at[t, k, core], zs.at[t, k, core], zr.at[t, k, core],
            device_id={"pts": partners[t]}, device_id_type=MESH,
        )

    def residual_copy(k, o, core):
        return pltpu.make_async_remote_copy(
            resid.at[k, core], gath.at[k, o], gs.at[k], gr.at[k],
            device_id=at_core(o, core), device_id_type=MESH,
        )

    def spread(k, core):
        each(1, m, lambda o: residual_copy(k, o, core).start())
        if core != owner:
            residual_copy(k, 0, core).start()

    @pl.when(owns)
    def _():
        for k, core in pieces:
            back = owner - core
            first = 0 if back else 1
            arrived = rbuf.at[k, back, pl.ds(first, m - first)]
            pltpu.make_async_copy(arrived, arrived, rr.at[k, back]).wait()
            acc = rbuf[k, back, 0] if back else part[k, 0]
            if m <= UNROLL:
                for o in range(1, m):
                    acc = acc + rbuf[k, back, o]
            else:
                acc = lax.fori_loop(1, m, lambda o, so_far: so_far + rbuf[k, back, o], acc)
            zsend[k, core] = acc
            for t in range(len(partners)):
                swap(k, core, t).start()

        energy = jnp.zeros((block, width), jnp.float32)
        for k, core in pieces:
            whole = zsend[k, core]
            for t in range(len(partners)):
                swap(k, core, t).wait_recv()
                whole = whole + zbuf[t, k, core]
            whole = whole.reshape(tiles, block, width)
            resid[k, core] = whole
            pl.when(side != last)(functools.partial(spread, k, core))
            energy = energy + jnp.sum(whole * whole, axis=0)
            if core == owner:
                gath[k, 0] = whole
        energy = jnp.sum(energy, axis=0, keepdims=True)

        @pl.when(side == last)
        def _():
            told[0] = energy
            ebuf[0] = energy

            def tell(o, own=False):
                for t in range(sides):
                    for core in range(nr):
                        if not (own and t == last and core == owner):
                            pltpu.make_async_remote_copy(
                                told.at[0], ebuf.at[o], es, er,
                                device_id={"pts": device_at(t, peer(o)), "rcv": core}, device_id_type=MESH,
                            ).start()

            each(1, m, tell)
            tell(0, own=True)
            for k, core in pieces:
                spread(k, core)

    def arrival(k, first):
        arrived = gath.at[k, pl.ds(first, m - first)]
        return pltpu.make_async_copy(arrived, arrived, gr.at[k])

    def energies(first):
        heard = ebuf.at[pl.ds(first, m - first)]
        return pltpu.make_async_copy(heard, heard, er)

    pl.when(tells)(energies(1).wait)
    pl.when(jnp.logical_not(tells))(energies(0).wait)
    summed = jnp.sum(jnp.sum(ebuf[pl.ds(0, m)], axis=0), axis=(0, 1), keepdims=True)
    spread_sq = summed / (sources * receivers * nr) + 1e-06
    inverse = 1.0 / spread_sq

    def gathered(g, h, part_of):
        return jnp.concatenate(
            [
                jnp.concatenate(
                    [
                        gath[k, g * group + i, 2 * t + part_of]
                        for i in range(group)
                        for t in range(sides)
                    ],
                    axis=0,
                )
                for k in range(h * per_half, (h + 1) * per_half)
            ],
            axis=1,
        )

    def image_of(g, h):
        at = pl.ds(h * half, half)
        real = gathered(g, h, 0)
        imag = gathered(g, h, 1)
        gain = 1.0 / (1.0 + (real * real + imag * imag) * inverse)
        weighted = jnp.concatenate([real * gain, imag * gain], axis=0)
        with_real = product(weighted, b_high[0, at], b_low[0, at], 0)
        with_imag = product(weighted, b_high[1, at], b_low[1, at], 0)
        back_real = with_real[:rows] + with_imag[rows:]
        back_imag = with_real[rows:] - with_imag[:rows]
        terms = rows_from(0, g * group, origin) * back_real + rows_from(1, g * group, origin) * back_imag
        return jnp.sum(terms, axis=0, keepdims=True)

    image = jnp.zeros((1, src.shape[2]), jnp.float32)
    for h in range(halves):
        for k in range(h * per_half, (h + 1) * per_half):
            pl.when(owns)(arrival(k, 1).wait)
            pl.when(jnp.logical_not(owns))(arrival(k, 0).wait)
        if m // group == 1:
            image = image + image_of(0, h)
        else:
            image = lax.fori_loop(0, m // group, lambda g, so_far: so_far + image_of(g, h), image)
    image = image * scale
    img[0] = image
    sums = []
    for d in range(1, nr):
        copy = pltpu.make_async_remote_copy(
            img.at[0], img_in.at[d - 1], ims.at[d - 1], imr.at[d - 1],
            device_id={"rcv": (c + d) % nr}, device_id_type=MESH,
        )
        copy.start()
        sums.append(copy)

    def sums_left(k, first):
        sent = part.at[k, pl.ds(first, m - first)]
        return pltpu.make_async_copy(sent, sent, rs.at[k])

    def residuals_left(k):
        sent = gath.at[k, pl.ds(0, m * nr - 1)]
        return pltpu.make_async_copy(sent, sent, gs.at[k])

    for k in range(chunks):
        pl.when(jnp.logical_not(owns))(sums_left(k, 0).wait)

    @pl.when(owns)
    def _():
        for k in range(chunks):
            sums_left(k, 1).wait()
            for core in range(nr):
                for t in range(len(partners)):
                    swap(k, core, t).wait_send()
            residuals_left(k).wait()

    @pl.when(tells)
    def _():
        every = ebuf.at[pl.ds(0, n * nr - 1)]
        pltpu.make_async_copy(every, every, es).wait()

    for copy in sums:
        copy.wait_recv()
    for d in range(1, nr):
        image = image + img_in[d - 1]
    out_ref[...] = image
    for copy in sums:
        copy.wait_send()


def local(src_green, rcv_green, model, observed):
    n = lax.axis_size("pts")
    nr = lax.axis_size("rcv")
    sources, points = src_green.shape[1:]
    receivers = rcv_green.shape[1]
    block = observed.shape[0]
    scale = math.sqrt(points * n / (receivers * nr * sources))
    f32, bf16 = jnp.float32, jnp.bfloat16
    dma = pltpu.SemaphoreType.DMA
    width = 128 if receivers % 256 == 0 else receivers
    chunks = receivers // width
    sides = 2 if n % 2 == 0 and n > 2 else 1
    m = n // sides
    blocks = (sides, 2, block, width)
    tiles = (2 * sides, block, width)
    image = pl.pallas_call(
        functools.partial(kernel, n, nr, scale),
        out_shape=jax.ShapeDtypeStruct((1, points), f32),
        in_specs=[pl.BlockSpec(memory_space=pl.ANY)] * 4,
        out_specs=pl.BlockSpec(memory_space=pltpu.VMEM),
        scratch_shapes=[
            pltpu.VMEM(src_green.shape, f32),
            pltpu.VMEM(rcv_green.shape, f32),
            pltpu.VMEM((1, points), f32),
            pltpu.VMEM(observed.shape, f32),
            pltpu.VMEM(rcv_green.shape, bf16),
            pltpu.VMEM(rcv_green.shape, bf16),
            pltpu.VMEM((chunks, m) + blocks, f32),
            pltpu.VMEM((chunks, nr, m) + blocks, f32),
            pltpu.VMEM((chunks, nr) + blocks, f32),
            pltpu.VMEM((max(sides - 1, 1), chunks, nr) + blocks, f32),
            pltpu.VMEM((chunks, nr) + tiles, f32),
            pltpu.VMEM((chunks, m * nr) + tiles, f32),
            pltpu.VMEM((chunks,) + blocks, f32),
            pltpu.VMEM((1, 1, width), f32),
            pltpu.VMEM((n * nr, 1, width), f32),
            pltpu.VMEM((1, 1, points), f32),
            pltpu.VMEM((max(nr - 1, 1), 1, points), f32),
            dma((3 + max(chunks, 2),)),
            dma((chunks,)),
            dma((chunks, nr)),
            dma((chunks,)),
            dma((chunks,)),
            dma((max(sides - 1, 1), chunks, nr)),
            dma((max(sides - 1, 1), chunks, nr)),
            dma(()),
            dma(()),
            dma((max(nr - 1, 1),)),
            dma((max(nr - 1, 1),)),
        ],
        compiler_params=pltpu.CompilerParams(collective_id=0, has_side_effects=True, vmem_limit_bytes=VMEM),
    )(src_green, rcv_green, model.reshape(1, points), observed)
    return image.reshape(points)


def solution(mesh):
    placed = (
        P(None, "grp", "pts"),
        P(None, ("grp", "rcv"), "pts"),
        P(("grp", "pts")),
        P(("grp", "pts"), None, "rcv"),
    )
    return jax.shard_map(
        local, mesh=mesh, in_specs=placed, out_specs=P(("grp", "pts")), check_vma=False
    )
```
